32 devices in a mesh: groups: 2 (over y), tok: 16 (over z, x, core).
Axes of the slice: x: 2, y: 2, z: 4, core: 2. Of those that a mesh axis runs over, the one named last changes fastest.
Arguments:
- activations: bfloat16 [2, 20480, 2048], P(None, ('groups', 'tok')), parts along dimension 1, may hold values from -6 to 6
- gradients: bfloat16 [2, 20480, 2048], P(None, ('groups', 'tok')), parts along dimension 1, may hold values from -6 to 6
- query_u: bfloat16 [4, 2048, 1024], P('groups', 'tok'), parts along dimension 0, may hold values from -4 to 4
- query_v: bfloat16 [4, 2048, 1024], P('groups', 'tok'), parts along dimension 0, may hold values from -4 to 4
- block_ids: int32 [4, 16], P('groups'), parts along dimension 0, may hold values from 0 to 31
- counts: int32 [32], P(('groups', 'tok')), parts along dimension 0, may hold values from 1 to 640, 5440 in all
Outputs:
- scores: float32 [20480, 64], P(('groups', 'tok')), parts along dimension 0
The draws below stay inside these ranges and needn't reach their ends.
There are 2 independent parts, one for each index of `groups`. The reference program is written for one: setup_inputs(seed, part) draws one part's arguments, and reference() takes and returns one part's arrays. A program takes and returns all parts, laid end to end along the dimension named above; each array names one. Nothing has to cross between parts.
Inputs may be any that keep to these rules, and one draw needn't show every extreme that they name: The counts of one part sum to (16 + 1) * 320 and the largest equals 640.
All inputs are finite; a program needn't handle non-finite values. No bound on the sum of `counts` on one device may be relied on, other than what follows from the above.
Results may differ from the reference program's by a relative error of at most 0.0003.
Values may be sent and summed in bfloat16 or wider, within the bound.
No kernel may reach another device: no remote copies, remote signals or barrier semaphores. Data moves between devices by JAX's collectives and lax.ppermute only.
A program may use at most 64 MiB of HBM per device.

```python
import math
import jax
import jax.numpy as jnp
import numpy as np
from jax import lax

D = 2048
LAYERS = 2
RANK = 8
QB = 4
NB = 16
BANK = 32
TOK_DEV = 640
NQ = 64
TOKENS = 10240
N_TOK = 16


def factor_drawn(key):
    keys = jax.random.split(key, 3)
    groups = BANK * QB
    common = jnp.clip(jax.random.normal(keys[0], (LAYERS, D, groups, 1), jnp.float32), -6.0, 6.0)
    own = jnp.clip(jax.random.normal(keys[1], (LAYERS, D, groups, RANK), jnp.float32), -6.0, 6.0)
    mixing = jax.random.uniform(keys[2], (LAYERS, 1, groups, 1), jnp.float32, 0.25, 0.6)
    values = (jnp.sqrt(mixing) * common + jnp.sqrt(1.0 - mixing) * own) * D ** (-0.5)
    return values.reshape(LAYERS, D, groups * RANK).astype(jnp.bfloat16)


def draw_query_u(key, part):
    inner = jax.random.fold_in(key, 11)
    return factor_drawn(inner)


def draw_query_v(key, part):
    inner = jax.random.fold_in(key, 23)
    return factor_drawn(inner)


def plant(values, rng, low, top_value):
    longest = values.shape.index(max(values.shape))
    spots = []
    for shift in (0, 1):
        where = [jax.random.randint(jax.random.fold_in(rng, axis), (), 0, length) for axis, length in enumerate(values.shape)]
        where[longest] = (where[longest] + shift) % values.shape[longest]
        spots.append(tuple(where))
    return values.at[spots[0]].set(low).at[spots[1]].set(top_value)


def level_of(stream_key, extent, cuts, smallest, high):
    level, own = 1.0, jax.random.fold_in(stream_key, 6)
    for position, parts in cuts:
        steps = jnp.exp(jax.random.uniform(jax.random.fold_in(own, position), (parts,), jnp.float32, smallest / len(cuts), high / len(cuts)))
        level = level * jnp.repeat(steps, extent[position] // parts).reshape([-1 if axis == position else 1 for axis in range(len(extent))])
    return level


def length_profile(amount, total, reach, skew):
    weights = [(1 << 20) // math.isqrt(standing ** skew) + 1 for standing in range(2, amount + 1)]
    spare, given = total - reach - (amount - 1), [1] * (amount - 1)
    while spare > 0:
        free = [i for i in range(amount - 1) if given[i] < reach]
        pool, budget = sum([weights[i] for i in free]), spare
        for i in free:
            addition = min(reach - given[i], max(1, budget * weights[i] // pool), spare)
            given[i] = given[i] + addition
            spare = spare - addition
    return np.array([reach] + given)


def uneven(key, count, total, limit, lean):
    if count == 2:
        one = jax.random.randint(key, (), max(1, total - limit), min(limit, total - 1) + 1)
        return jnp.stack([one, total - one])
    lengths = jnp.asarray(length_profile(count, total, limit, lean), jnp.int32)
    pairs = (count - 1) // 2
    giver, taker = lengths[1:1 + 2 * pairs:2], lengths[2:2 + 2 * pairs:2]
    margin = jnp.minimum(giver - 1, limit - taker)
    moved = jax.random.randint(jax.random.fold_in(key, 1), (pairs,), 0, 1 << 20) % (margin + 1)
    lengths = lengths.at[1:1 + 2 * pairs:2].set(giver - moved).at[2:2 + 2 * pairs:2].set(taker + moved)
    return lengths[jax.random.permutation(jax.random.fold_in(key, 2), count)]


def scatter_about(own_key, dims, spread, most, cuts=(), kind=jnp.bfloat16):
    gain = level_of(own_key, dims, cuts, -0.22, 0.18) if cuts else 1.0
    entries = jax.random.normal(own_key, dims, jnp.float32) * spread * gain
    return jnp.minimum(jnp.maximum(entries, -most), most).astype(kind)


def setup_inputs(seed: int = 0, part: int = 0) -> dict:
    seeds = jax.random.split(jax.random.key(seed), 7)
    own_keys = jax.random.split(jax.random.fold_in(seeds[6], part), 7)
    return {
        "activations": scatter_about(own_keys[0], (LAYERS, TOKENS, D), 1.0, 6.0, ((1, 16),)),
        "gradients": scatter_about(own_keys[1], (LAYERS, TOKENS, D), 1.0, 6.0, ((1, 16),)),
        "query_u": draw_query_u(jax.random.fold_in(jax.random.fold_in(seeds[6], part), 71), part),
        "query_v": draw_query_v(jax.random.fold_in(jax.random.fold_in(seeds[6], part), 71), part),
        "block_ids": plant(jax.random.randint(own_keys[4], (LAYERS, NB), 0, BANK), jax.random.fold_in(own_keys[4], 1), 0, BANK - 1).astype(jnp.int32),
        "counts": uneven(own_keys[5], N_TOK, (N_TOK + 1) * TOK_DEV // 2, TOK_DEV, 2).astype(jnp.int32),
    }


def pick_columns(factor, block_ids):
    width = QB * RANK
    chosen = []
    for layer in range(factor.shape[0]):
        slots = factor[layer].reshape(factor.shape[1], -1, width)
        chosen.append(jnp.take(slots, block_ids[layer].astype(jnp.int32), axis=1).reshape(factor.shape[1], -1))
    return jnp.stack(chosen)

def rank_grams(factor):
    per = factor.astype(jnp.float32).reshape(factor.shape[0], factor.shape[1], -1, RANK)
    return jnp.einsum('lkqr,lkqs->lqrs', per, per)

def reference(activations, gradients, query_u, query_v, block_ids, counts):
    chosen_u = pick_columns(query_u, block_ids)
    chosen_v = pick_columns(query_v, block_ids)
    raw = jnp.zeros((TOKENS, NQ), jnp.float32)
    for layer in range(LAYERS):
        grad_proj = jnp.dot(gradients[layer], chosen_u[layer], preferred_element_type=jnp.float32)
        act_proj = jnp.dot(activations[layer], chosen_v[layer], preferred_element_type=jnp.float32)
        raw = raw + lax.optimization_barrier(jnp.sum((grad_proj * act_proj).reshape(TOKENS, NQ, RANK), axis=2))
    norm_sq = lax.optimization_barrier(jnp.sum(rank_grams(chosen_u) * rank_grams(chosen_v), axis=(0, 2, 3)))
    slot = jnp.arange(TOKENS, dtype=jnp.int32)
    owner = slot // TOK_DEV
    live = slot % TOK_DEV < counts[owner]
    scaled = raw / jnp.sqrt(norm_sq + 1e-06)[None, :]
    return jnp.where(live[:, None], scaled, jnp.zeros_like(scaled))
```

```python
import functools

import jax
import jax.numpy as jnp
from jax import lax
from jax.experimental import pallas as pl
from jax.experimental.pallas import tpu as pltpu
from jax.sharding import PartitionSpec as P

RANK = 8
QB = 4
OUTER = 4
LANES = 128
TILE = 256


def pick_columns(factor, block_ids):
    width = QB * RANK
    chosen = []
    for layer in range(factor.shape[0]):
        slots = factor[layer].reshape(factor.shape[1], -1, width)
        chosen.append(jnp.take(slots, block_ids[layer], axis=1).reshape(factor.shape[1], -1))
    return jnp.stack(chosen)


def rank_grams(factor):
    per = factor.reshape(factor.shape[0], factor.shape[1], -1, RANK)
    return jnp.einsum("lkqr,lkqs->lqrs", per, per, preferred_element_type=jnp.float32)


def per_device_plain(activations, gradients, query_u, query_v, block_ids, counts):
    layers, tok_rows, width = activations.shape
    columns = block_ids.shape[1] * QB * RANK
    queries = columns // RANK
    whole_u = lax.all_gather(pick_columns(query_u, block_ids), "tok", axis=1, tiled=True)
    whole_v = lax.all_gather(pick_columns(query_v, block_ids), "tok", axis=1, tiled=True)
    grad_proj = jnp.einsum("ltk,lkc->ltc", gradients, whole_u, preferred_element_type=jnp.float32)
    act_proj = jnp.einsum("ltk,lkc->ltc", activations, whole_v, preferred_element_type=jnp.float32)
    raw = jnp.sum((grad_proj * act_proj).reshape(layers, tok_rows, queries, RANK), axis=(0, 3))
    norm_sq = jnp.sum(rank_grams(whole_u) * rank_grams(whole_v), axis=(0, 2, 3))
    live = jnp.arange(tok_rows, dtype=jnp.int32) < counts[0]
    scaled = raw / jnp.sqrt(norm_sq + 1e-06)[None, :]
    return jnp.where(live[:, None], scaled, jnp.zeros_like(scaled))


def pick_kernel(layer, ids_ref, u_ref, v_ref, out_ref):
    width = QB * RANK
    rows, bank = u_ref.shape
    columns = out_ref.shape[2]
    lane = lax.broadcasted_iota(jnp.int32, (1, columns), 1)
    target = jnp.zeros((1, columns), jnp.int32)
    for block in range(columns // width):
        target = jnp.where(lane // width == block, ids_ref[layer, block] * width, target)
    target = target + lane % width
    row = lax.broadcasted_iota(jnp.int32, (bank, columns), 0)
    chooser = jnp.where(row == target, 1.0, 0.0).astype(jnp.bfloat16)
    both = jnp.concatenate([u_ref[...], v_ref[...]], axis=0)
    got = jnp.dot(both, chooser, preferred_element_type=jnp.float32).astype(jnp.bfloat16)
    out_ref[0] = got[:rows]
    out_ref[1] = got[rows:]


def pick(layer, query_u, query_v, block_ids):
    layers, rows, bank = query_u.shape
    columns = block_ids.shape[1] * QB * RANK
    spec = pl.BlockSpec((None, rows, bank), lambda i: (layer, 0, 0))
    return pl.pallas_call(
        functools.partial(pick_kernel, layer),
        out_shape=jax.ShapeDtypeStruct((2, rows, columns), jnp.bfloat16),
        grid=(1,),
        in_specs=[pl.BlockSpec(memory_space=pltpu.SMEM), spec, spec],
        out_specs=pl.BlockSpec((2, rows, columns), lambda i: (0, 0, 0)),
        cost_estimate=pl.CostEstimate(
            flops=4 * rows * bank * columns, bytes_accessed=4 * rows * (bank + columns), transcendentals=0
        ),
        name=f"pick{layer}",
    )(block_ids, query_u, query_v)


def split_dot(left, right):
    total = None
    rest = left
    for _ in range(3):
        term = rest.astype(jnp.bfloat16)
        rest = rest - term.astype(jnp.float32)
        part = jnp.dot(term, right, preferred_element_type=jnp.float32)
        total = part if total is None else total + part
    return total


def group_sums(columns):
    row = lax.broadcasted_iota(jnp.int32, (columns, columns // RANK), 0)
    col = lax.broadcasted_iota(jnp.int32, (columns, columns // RANK), 1)
    return jnp.where(row // RANK == col, 1.0, 0.0).astype(jnp.bfloat16)


def source_rows(shape, where):
    outer, inner = shape
    me = lax.axis_index("tok")
    a, b, c = me // (2 * inner), (me // 2) % inner, me % 2
    da, db, dc = where
    return (((a + outer - da) % outer) * inner + (b + inner - db) % inner) * 2 + (c + dc) % 2


def stage_kernel(cfg, *refs):
    shape, groups, last = cfg["shape"], cfg["groups"], cfg["last"]
    refs = list(refs)
    take = lambda n: [refs.pop(0) for _ in range(n)]
    (xg_ref, xa_ref) = take(2)
    extra = take(cfg["extra"])
    pieces = [take(len(g["where"])) for g in groups]
    starts = [take(3) if g["carry"] else None for g in groups]
    outs = take(1) if last == "all" else (take(2) if last == "layer" else take(3 * len(groups)))
    xg, xa, w, sems = take(4)
    rows = w.shape[2] // max(1, 1)
    at, copies = 0, []
    slot = 0
    for g, arrays in zip(groups, pieces):
        these = []
        for n, (where, array) in enumerate(zip(g["where"], arrays)):
            start = pl.multiple_of(source_rows(shape, where) * cfg["rows"], LANES)
            span = pl.ds(slot * cfg["rows"], cfg["rows"])
            cg = pltpu.make_async_copy(
                xg_ref.at[g["layer"], :, pl.ds(start, cfg["rows"])], xg.at[:, span], sems.at[3 * slot]
            )
            ca = pltpu.make_async_copy(
                xa_ref.at[g["layer"], :, pl.ds(start, cfg["rows"])], xa.at[:, span], sems.at[3 * slot + 1]
            )
            cw = pltpu.make_async_copy(array, w.at[:, span, :], sems.at[3 * slot + 2])
            for copy in (cw, cg, ca):
                copy.start()
            these.append((cw, cg, ca))
            slot += 1
        copies.append(these)
    columns = w.shape[2]
    tiles = columns // TILE
    product = None
    norm = None
    slot = 0
    for index, (g, these) in enumerate(zip(groups, copies)):
        for copy_set in these:
            for copy in copy_set:
                copy.wait()
        span = pl.ds(slot * cfg["rows"], len(these) * cfg["rows"])
        slot += len(these)
        proj = [
            jnp.dot(x[:, span], w[s, span, :], preferred_element_type=jnp.float32)
            for s, x in ((0, xg), (1, xa))
        ]
        grams = []
        for s in range(2):
            for t in range(tiles):
                part = w[s, span, t * TILE : (t + 1) * TILE]
                grams.append(
                    lax.dot_general(part, part, (((0,), (0,)), ((), ())), preferred_element_type=jnp.float32)
                )
        if starts[index] is not None:
            pg, pa, gr = starts[index]
            proj = [proj[0] + pg[...], proj[1] + pa[...]]
            grams = [gram + gr[i] for i, gram in enumerate(grams)]
        if last is None:
            og, oa, ogr = outs[3 * index : 3 * index + 3]
            og[...] = proj[0]
            oa[...] = proj[1]
            for i, gram in enumerate(grams):
                ogr[i] = gram
        else:
            term = proj[0] * proj[1]
            product = term if product is None else product + term
            row = lax.broadcasted_iota(jnp.int32, (TILE, TILE), 0)
            col = lax.broadcasted_iota(jnp.int32, (TILE, TILE), 1)
            same = row // RANK == col // RANK
            sums = [
                jnp.sum(jnp.where(same, grams[t] * grams[tiles + t], 0.0), axis=0, keepdims=True)
                for t in range(tiles)
            ]
            sums = jnp.concatenate(sums, axis=1)
            norm = sums if norm is None else norm + sums
    if last == "all":
        counts_ref = extra[0]
        chooser = group_sums(columns)
        raw = split_dot(product, chooser)
        norm = split_dot(jnp.broadcast_to(norm, (8, columns)), chooser)[:1]
        scaled = raw / jnp.sqrt(norm + 1e-06)
        token = lax.broadcasted_iota(jnp.int32, scaled.shape, 0)
        outs[0][...] = jnp.where(token < counts_ref[0], scaled, 0.0)


def stage(shape, groups, gradients, activations, last=None, counts=None, name="stage"):
    rows, columns = groups[0]["arrays"][0].shape[1:]
    tokens = gradients.shape[1]
    slots = sum(len(g["where"]) for g in groups)
    tiles = 2 * (columns // TILE)
    anywhere = pl.BlockSpec(memory_space=pl.ANY)
    vmem = pl.BlockSpec(memory_space=pltpu.VMEM)
    args, specs = [gradients, activations], [anywhere, anywhere]
    if last == "all":
        args.append(counts)
        specs.append(pl.BlockSpec(memory_space=pltpu.SMEM))
    for g in groups:
        args += g["arrays"]
        specs += [anywhere] * len(g["arrays"])
    for g in groups:
        if g["carry"] is not None:
            args += list(g["carry"])
            specs += [vmem] * 3
    proj = jax.ShapeDtypeStruct((tokens, columns), jnp.float32)
    gram = jax.ShapeDtypeStruct((tiles, TILE, TILE), jnp.float32)
    if last == "all":
        out_shape = jax.ShapeDtypeStruct((tokens, columns // RANK), jnp.float32)
        out_specs = vmem
    else:
        out_shape = (proj, proj, gram) * len(groups)
        out_specs = (vmem,) * len(out_shape)
    cfg = dict(
        shape=shape,
        rows=rows,
        last=last,
        extra=1 if last == "all" else 0,
        groups=[dict(layer=g["layer"], where=g["where"], carry=g["carry"] is not None) for g in groups],
    )
    flops = 2 * slots * rows * columns * (2 * tokens + tiles * TILE)
    return pl.pallas_call(
        functools.partial(stage_kernel, cfg),
        out_shape=out_shape,
        in_specs=specs,
        out_specs=out_specs,
        scratch_shapes=[
            pltpu.VMEM((tokens, slots * rows), jnp.bfloat16),
            pltpu.VMEM((tokens, slots * rows), jnp.bfloat16),
            pltpu.VMEM((2, slots * rows, columns), jnp.bfloat16),
            pltpu.SemaphoreType.DMA((3 * slots,)),
        ],
        compiler_params=pltpu.CompilerParams(vmem_limit_bytes=48 << 20),
        cost_estimate=pl.CostEstimate(
            flops=flops, bytes_accessed=4 * slots * rows * (tokens + columns), transcendentals=0
        ),
        name=name,
    )(*args)


def after(value, *others):
    return lax.optimization_barrier((value,) + others)[0]


def per_device(shape, activations, gradients, query_u, query_v, block_ids, counts):
    outer, inner = shape

    def number(a, b, c):
        return ((a % outer) * inner + b % inner) * 2 + c % 2

    def steps(da, db, dc):
        return [
            (number(a, b, c), number(a + da, b + db, c + dc))
            for a in range(outer)
            for b in range(inner)
            for c in range(2)
        ]

    def move(value, da, db, dc):
        return lax.ppermute(value, "tok", steps(da, db, dc))

    have = [{}, {}]
    own = [pick(0, query_u, query_v, block_ids), None]
    have[0][(0, 0)] = own[0]
    x_of = [{}, {}]
    have[0][(0, 1)] = move(own[0], 0, 1, 0)
    have[0][(1, 0)] = move(own[0], 1, 0, 0)
    own[1] = pick(1, query_u, query_v, block_ids)
    have[1][(0, 0)] = own[1]
    have[1][(0, 1)] = move(own[1], 0, 1, 0)
    have[1][(1, 0)] = move(own[1], 1, 0, 0)
    for da in range(1, outer):
        for layer in range(2):
            h = have[layer]
            final = da == outer - 1
            if not final:
                fed = after(h[(da, 0)], h[(da - 1, 1)])
                h[(da + 1, 0)] = move(fed, 1, 0, 0)
            if final and layer == 1:
                fed = after(h[(0, 1)], h[(da, 0)])
                h[(da, 1)] = move(fed, -1, 0, 0)
            else:
                h[(da, 1)] = move(h[(da, 0)], 0, 1, 0)

    def both_cores(layer, keys):
        where, arrays = [], []
        for da, db in keys:
            piece = have[layer][(da, db)]
            where += [(da, db, 0), (da, db, 1)]
            arrays += [piece, move(piece, 0, 0, 1)]
        return dict(layer=layer, where=where, arrays=arrays)

    early = [(0, 0), (0, 1), (1, 0), (1, 1), (2, 0)]
    middle = [(2, 1), (3, 0)]
    late = [(3, 1)]
    carry = [None, None]
    for layer in range(2):
        carry[layer] = stage(
            shape, [dict(both_cores(layer, early), carry=None)], gradients, activations, name=f"early{layer}"
        )
    for layer in range(2):
        carry[layer] = stage(
            shape,
            [dict(both_cores(layer, middle), carry=carry[layer])],
            gradients,
            activations,
            name=f"middle{layer}",
        )
    return stage(
        shape,
        [dict(both_cores(layer, late), carry=carry[layer]) for layer in range(2)],
        gradients,
        activations,
        last="all",
        counts=counts,
        name="finish",
    )


def solution(mesh):
    spec = (
        P(None, ("groups", "tok"), None),
        P(None, ("groups", "tok"), None),
        P("groups", "tok", None),
        P("groups", "tok", None),
        P("groups", None),
        P(("groups", "tok")),
    )
    members = mesh.shape["tok"]
    shape = (OUTER, members // (2 * OUTER))

    def whole(activations, gradients, query_u, query_v, block_ids, counts):
        rows = query_u.shape[1] // members
        fits = members == 4 * OUTER and rows % LANES == 0
        body = functools.partial(per_device, shape) if fits else per_device_plain
        return jax.shard_map(
            body,
            mesh=mesh,
            in_specs=spec,
            out_specs=P(("groups", "tok"), None),
            check_vma=False,
        )(activations, gradients, query_u, query_v, block_ids, counts)

    return whole
```

```python
import functools

import jax
import jax.numpy as jnp
from jax import lax
from jax.experimental import pallas as pl
from jax.experimental.pallas import tpu as pltpu
from jax.sharding import PartitionSpec as P


RANK = 8
QB = 4
OUTER = 4
LANES = 128
TILE = 256


def pick_columns(factor, block_ids):
    width = QB * RANK
    chosen = []
    for layer in range(factor.shape[0]):
        slots = factor[layer].reshape(factor.shape[1], -1, width)
        chosen.append(jnp.take(slots, block_ids[layer], axis=1).reshape(factor.shape[1], -1))
    return jnp.stack(chosen)


def rank_grams(factor):
    per = factor.reshape(factor.shape[0], factor.shape[1], -1, RANK)
    return jnp.einsum("lkqr,lkqs->lqrs", per, per, preferred_element_type=jnp.float32)


def per_device_plain(activations, gradients, query_u, query_v, block_ids, counts):
    layers, tok_rows, _ = activations.shape
    columns = block_ids.shape[1] * QB * RANK
    queries = columns // RANK
    whole_u = lax.all_gather(pick_columns(query_u, block_ids), "tok", axis=1, tiled=True)
    whole_v = lax.all_gather(pick_columns(query_v, block_ids), "tok", axis=1, tiled=True)
    grad_proj = jnp.einsum("ltk,lkc->ltc", gradients, whole_u, preferred_element_type=jnp.float32)
    act_proj = jnp.einsum("ltk,lkc->ltc", activations, whole_v, preferred_element_type=jnp.float32)
    raw = jnp.sum((grad_proj * act_proj).reshape(layers, tok_rows, queries, RANK), axis=(0, 3))
    norm_sq = jnp.sum(rank_grams(whole_u) * rank_grams(whole_v), axis=(0, 2, 3))
    live = jnp.arange(tok_rows, dtype=jnp.int32) < counts[0]
    scaled = raw / jnp.sqrt(norm_sq + 1e-06)[None, :]
    return jnp.where(live[:, None], scaled, jnp.zeros_like(scaled))


def pick_kernel(layer, ids_ref, u_ref, v_ref, out_ref, held, sems):
    width = QB * RANK
    rows, bank = u_ref.shape[1:]
    columns = out_ref.shape[2]
    copies = [
        pltpu.make_async_copy(ref.at[layer], held.at[pl.ds(s * rows, rows), :], sems.at[s])
        for s, ref in enumerate((u_ref, v_ref))
    ]
    for copy in copies:
        copy.start()
    lane = lax.broadcasted_iota(jnp.int32, (1, columns), 1)
    named = jnp.zeros((1, columns), jnp.int32)
    for block in range(columns // width):
        named = jnp.where(lane // width == block, ids_ref[layer, block], named)
    row = lax.broadcasted_iota(jnp.int32, (width, columns), 0)
    col = lax.broadcasted_iota(jnp.int32, (width, columns), 1) % width
    one = jnp.where(row == col, 1.0, 0.0).astype(jnp.bfloat16)
    chooser = [
        one * jnp.where(named == stored, 1.0, 0.0).astype(jnp.bfloat16) for stored in range(bank // width)
    ]
    chooser = jnp.concatenate(chooser, axis=0)
    for copy in copies:
        copy.wait()
    got = jnp.dot(held[...], chooser, preferred_element_type=jnp.float32).astype(jnp.bfloat16)
    out_ref[0] = got[:rows]
    out_ref[1] = got[rows:]


def pick(layer, query_u, query_v, block_ids):
    _, rows, bank = query_u.shape
    columns = block_ids.shape[1] * QB * RANK
    return pl.pallas_call(
        functools.partial(pick_kernel, layer),
        out_shape=jax.ShapeDtypeStruct((2, rows, columns), jnp.bfloat16),
        in_specs=[pl.BlockSpec(memory_space=pltpu.SMEM)] + [pl.BlockSpec(memory_space=pltpu.HBM)] * 2,
        out_specs=pl.BlockSpec(memory_space=pltpu.VMEM),
        scratch_shapes=[pltpu.VMEM((2 * rows, bank), jnp.bfloat16), pltpu.SemaphoreType.DMA((2,))],
        cost_estimate=pl.CostEstimate(
            flops=4 * rows * bank * columns, bytes_accessed=4 * rows * (bank + columns), transcendentals=0
        ),
    )(block_ids, query_u, query_v)


def split_dot(left, right):
    total = None
    rest = left
    for _ in range(3):
        term = rest.astype(jnp.bfloat16)
        rest = rest - term.astype(jnp.float32)
        part = jnp.dot(term, right, preferred_element_type=jnp.float32)
        total = part if total is None else total + part
    return total


def group_sums(columns):
    row = lax.broadcasted_iota(jnp.int32, (columns, LANES), 0)
    col = lax.broadcasted_iota(jnp.int32, (columns, LANES), 1)
    return jnp.where(row // RANK == col, 1.0, 0.0).astype(jnp.bfloat16)


def stage_kernel(cfg, *refs):
    (outer, inner), groups, last, rows = cfg["shape"], cfg["groups"], cfg["last"], cfg["rows"]
    refs = list(refs)

    def take(n):
        return [refs.pop(0) for _ in range(n)]

    x_refs = take(2)
    counts_ref = take(1)[0] if last else None
    pieces = [[take(2) for _ in g["where"]] for g in groups]
    starts = [take(3) if g["carry"] else None for g in groups]
    outs = take(1) if last else None
    totals = [take(3) for _ in groups]
    x, w, sems = take(3)
    me = lax.axis_index("tok")
    a, b, c = me // (2 * inner), (me // 2) % inner, me % 2
    copies, slot = [], 0
    for g, arrays in zip(groups, pieces):
        for (da, db), pair in zip(g["where"], arrays):
            owner = ((a + outer - da) % outer) * inner + (b + inner - db) % inner
            start = pl.multiple_of(owner * 2 * rows, LANES)
            these = []
            for dc, array in enumerate(pair):
                spot = pl.multiple_of(slot * 2 * rows + ((c + dc) % 2) * rows, LANES)
                these.append((array, w.at[:, pl.ds(spot, rows), :]))
            for s, x_ref in enumerate(x_refs):
                these.append((x_ref.at[g["layer"], :, pl.ds(start, 2 * rows)], x.at[slot, s]))
            these = [pltpu.make_async_copy(*ends, sems.at[4 * slot + i]) for i, ends in enumerate(these)]
            for copy in these:
                copy.start()
            copies.append(these)
            slot += 1
    tiles = w.shape[2] // TILE
    slot = 0
    for g, start, total in zip(groups, starts, totals):
        for first in range(len(g["where"])):
            for copy in copies[slot]:
                copy.wait()
            span = slice(slot * 2 * rows, (slot + 1) * 2 * rows)
            came = start if first == 0 else total
            for s in range(2):
                part = jnp.dot(x[slot, s], w[s, span, :], preferred_element_type=jnp.float32)
                total[s][...] = part if came is None else came[s][...] + part
            for s in range(2):
                for t in range(tiles):
                    one = w[s, span, t * TILE : (t + 1) * TILE]
                    part = lax.dot_general(one, one, (((0,), (0,)), ((), ())), preferred_element_type=jnp.float32)
                    i = s * tiles + t
                    total[2][i] = part if came is None else came[2][i] + part
            slot += 1
    if last:
        columns = w.shape[2]
        row = lax.broadcasted_iota(jnp.int32, (TILE, TILE), 0)
        col = lax.broadcasted_iota(jnp.int32, (TILE, TILE), 1)
        same = row // RANK == col // RANK
        norm = []
        for t in range(tiles):
            both = sum(total[2][t] * total[2][tiles + t] for total in totals)
            norm.append(jnp.sum(jnp.where(same, both, 0.0), axis=0, keepdims=True))
        norm = jnp.broadcast_to(jnp.concatenate(norm, axis=1), (8, columns))
        chooser = group_sums(columns)
        norm = split_dot(norm, chooser)[:1]
        raw = split_dot(sum(total[0][...] * total[1][...] for total in totals), chooser)
        scaled = raw / jnp.sqrt(norm + 1e-06)
        token = lax.broadcasted_iota(jnp.int32, scaled.shape, 0)
        scaled = jnp.where(token < counts_ref[0], scaled, 0.0)
        outs[0][...] = scaled.T[: columns // RANK]


def stage(shape, groups, gradients, activations, counts=None):
    last = counts is not None
    rows, columns = groups[0]["arrays"][0][0].shape[1:]
    tokens = gradients.shape[1]
    slots = sum(len(g["where"]) for g in groups)
    tiles = 2 * (columns // TILE)
    anywhere = pl.BlockSpec(memory_space=pltpu.HBM)
    vmem = pl.BlockSpec(memory_space=pltpu.VMEM)
    args, specs = [gradients, activations], [anywhere, anywhere]
    if last:
        args.append(counts)
        specs.append(pl.BlockSpec(memory_space=pltpu.SMEM))
    for g in groups:
        for pair in g["arrays"]:
            args += pair
            specs += [anywhere] * 2
    aliases = {}
    for n, g in enumerate(groups):
        if g["carry"] is not None:
            if not last:
                aliases.update({len(args) + i: 3 * n + i for i in range(3)})
            args += list(g["carry"])
            specs += [vmem] * 3
    sums = [((tokens, columns), jnp.float32)] * 2 + [((tiles, TILE, TILE), jnp.float32)]
    scratch = []
    if last:
        out_shape = jax.ShapeDtypeStruct((columns // RANK, tokens), jnp.float32)
        out_specs = vmem
        scratch = [pltpu.VMEM(*one) for one in sums] * len(groups)
    else:
        out_shape = tuple(jax.ShapeDtypeStruct(*one) for one in sums) * len(groups)
        out_specs = (vmem,) * len(out_shape)
    cfg = dict(
        shape=shape,
        rows=rows,
        last=last,
        groups=[dict(layer=g["layer"], where=g["where"], carry=g["carry"] is not None) for g in groups],
    )
    flops = 4 * slots * rows * columns * (2 * tokens + tiles * TILE)
    return pl.pallas_call(
        functools.partial(stage_kernel, cfg),
        out_shape=out_shape,
        in_specs=specs,
        out_specs=out_specs,
        scratch_shapes=scratch
        + [
            pltpu.VMEM((slots, 2, tokens, 2 * rows), jnp.bfloat16),
            pltpu.VMEM((2, slots * 2 * rows, columns), jnp.bfloat16),
            pltpu.SemaphoreType.DMA((4 * slots,)),
        ],
        input_output_aliases=aliases,
        compiler_params=pltpu.CompilerParams(vmem_limit_bytes=52 << 20),
        cost_estimate=pl.CostEstimate(
            flops=flops, bytes_accessed=8 * slots * rows * (tokens + columns), transcendentals=0
        ),
    )(*args)


def after(value, *others):
    return lax.optimization_barrier((value,) + others)[0]


def per_device(shape, activations, gradients, query_u, query_v, block_ids, counts):
    outer, inner = shape

    def number(a, b, c):
        return ((a % outer) * inner + b % inner) * 2 + c % 2

    def move(value, da, db, dc):
        steps = [
            (number(a, b, c), number(a + da, b + db, c + dc))
            for a in range(outer)
            for b in range(inner)
            for c in range(2)
        ]
        return lax.ppermute(value, "tok", steps)

    have, pairs = [{}, {}], [{}, {}]
    for layer in range(2):
        have[layer][(0, 0)] = pick(layer, query_u, query_v, block_ids)
    for da in range(outer):
        for layer in range(2):
            h = have[layer]
            if da < outer - 1:
                fed = h[(da, 0)]
                if da:
                    fed = after(fed, h[(da - 1, 1)])
                h[(da + 1, 0)] = move(fed, 1, 0, 0)
            if da == outer - 1 and layer == 1:
                fed = after(h[(0, 1)], h[(da, 0)])
                h[(da, 1)] = move(fed, -1, 0, 0)
            else:
                h[(da, 1)] = move(h[(da, 0)], 0, 1, 0)
    for layer in range(2):
        for key, piece in have[layer].items():
            pairs[layer][key] = [piece, move(piece, 0, 0, 1)]

    def group(layer, keys, carry):
        return dict(layer=layer, where=keys, arrays=[pairs[layer][key] for key in keys], carry=carry)

    parts = [[(0, 0), (0, 1), (1, 0)]] + [[(da, 1), (da + 1, 0)] for da in range(1, outer - 1)]
    carry = [None, None]
    for keys in parts:
        for layer in range(2):
            carry[layer] = stage(shape, [group(layer, keys, carry[layer])], gradients, activations)
    scores = stage(
        shape,
        [group(layer, [(outer - 1, 1)], carry[layer]) for layer in range(2)],
        gradients,
        activations,
        counts=counts,
    )
    return scores.T


def solution(mesh):
    spec = (
        P(None, ("groups", "tok"), None),
        P(None, ("groups", "tok"), None),
        P("groups", "tok", None),
        P("groups", "tok", None),
        P("groups", None),
        P(("groups", "tok")),
    )
    members = mesh.shape["tok"]
    shape = (OUTER, members // (2 * OUTER))
    ring = members == 4 * OUTER

    def body(*args):
        fits = ring and args[2].shape[1] % LANES == 0
        return per_device(shape, *args) if fits else per_device_plain(*args)

    return jax.shard_map(body, mesh=mesh, in_specs=spec, out_specs=P(("groups", "tok"), None), check_vma=False)
```

```python
import functools

import jax
import jax.numpy as jnp
from jax import lax
from jax.experimental import pallas as pl
from jax.experimental.pallas import tpu as pltpu
from jax.sharding import PartitionSpec as P


RANK = 8
QB = 4
OUTER = 4
LANES = 128
TILE = 256


def pick_columns(factor, block_ids):
    width = QB * RANK
    chosen = []
    for layer in range(factor.shape[0]):
        slots = factor[layer].reshape(factor.shape[1], -1, width)
        chosen.append(jnp.take(slots, block_ids[layer], axis=1).reshape(factor.shape[1], -1))
    return jnp.stack(chosen)


def rank_grams(factor):
    per = factor.reshape(factor.shape[0], factor.shape[1], -1, RANK)
    return jnp.einsum("lkqr,lkqs->lqrs", per, per, preferred_element_type=jnp.float32)


def per_device_plain(activations, gradients, query_u, query_v, block_ids, counts):
    layers, tok_rows, _ = activations.shape
    columns = block_ids.shape[1] * QB * RANK
    queries = columns // RANK
    whole_u = lax.all_gather(pick_columns(query_u, block_ids), "tok", axis=1, tiled=True)
    whole_v = lax.all_gather(pick_columns(query_v, block_ids), "tok", axis=1, tiled=True)
    grad_proj = jnp.einsum("ltk,lkc->ltc", gradients, whole_u, preferred_element_type=jnp.float32)
    act_proj = jnp.einsum("ltk,lkc->ltc", activations, whole_v, preferred_element_type=jnp.float32)
    raw = jnp.sum((grad_proj * act_proj).reshape(layers, tok_rows, queries, RANK), axis=(0, 3))
    norm_sq = jnp.sum(rank_grams(whole_u) * rank_grams(whole_v), axis=(0, 2, 3))
    live = jnp.arange(tok_rows, dtype=jnp.int32) < counts[0]
    scaled = raw / jnp.sqrt(norm_sq + 1e-06)[None, :]
    return jnp.where(live[:, None], scaled, jnp.zeros_like(scaled))


def pick_kernel(layer, ids_ref, u_ref, v_ref, out_ref, held, sems):
    width = QB * RANK
    rows, bank = u_ref.shape[1:]
    columns = out_ref.shape[2]
    copies = [
        pltpu.make_async_copy(ref.at[layer], held.at[pl.ds(s * rows, rows), :], sems.at[s])
        for s, ref in enumerate((u_ref, v_ref))
    ]
    for copy in copies:
        copy.start()
    lane = lax.broadcasted_iota(jnp.int32, (1, columns), 1)
    named = jnp.zeros((1, columns), jnp.int32)
    for block in range(columns // width):
        named = jnp.where(lane // width == block, ids_ref[layer, block], named)
    row = lax.broadcasted_iota(jnp.int32, (width, columns), 0)
    col = lax.broadcasted_iota(jnp.int32, (width, columns), 1) % width
    aim = jnp.where(row == col, named, -1)
    chooser = [jnp.where(aim == stored, 1.0, 0.0).astype(jnp.bfloat16) for stored in range(bank // width)]
    chooser = jnp.concatenate(chooser, axis=0)
    for copy in copies:
        copy.wait()
    got = jnp.dot(held[...], chooser, preferred_element_type=jnp.float32).astype(jnp.bfloat16)
    out_ref[0] = got[:rows]
    out_ref[1] = got[rows:]


def pick(layer, query_u, query_v, block_ids):
    _, rows, bank = query_u.shape
    columns = block_ids.shape[1] * QB * RANK
    return pl.pallas_call(
        functools.partial(pick_kernel, layer),
        out_shape=jax.ShapeDtypeStruct((2, rows, columns), jnp.bfloat16),
        in_specs=[pl.BlockSpec(memory_space=pltpu.SMEM)] + [pl.BlockSpec(memory_space=pltpu.HBM)] * 2,
        out_specs=pl.BlockSpec(memory_space=pltpu.VMEM),
        scratch_shapes=[pltpu.VMEM((2 * rows, bank), jnp.bfloat16), pltpu.SemaphoreType.DMA((2,))],
        cost_estimate=pl.CostEstimate(
            flops=4 * rows * bank * columns, bytes_accessed=4 * rows * (bank + columns), transcendentals=0
        ),
    )(block_ids, query_u, query_v)


def load_kernel(*refs):
    half = len(refs) // 2
    sems = refs[-1]
    copies = [pltpu.make_async_copy(refs[i], refs[half + i], sems.at[i]) for i in range(half)]
    for copy in copies:
        copy.start()
    for copy in copies:
        copy.wait()


def load(*arrays):
    return pl.pallas_call(
        load_kernel,
        out_shape=tuple(jax.ShapeDtypeStruct(one.shape, one.dtype) for one in arrays),
        in_specs=[pl.BlockSpec(memory_space=pltpu.HBM)] * len(arrays),
        out_specs=(pl.BlockSpec(memory_space=pltpu.VMEM),) * len(arrays),
        scratch_shapes=[pltpu.SemaphoreType.DMA((len(arrays),))],
        compiler_params=pltpu.CompilerParams(vmem_limit_bytes=51 << 20),
        name="load",
    )(*arrays)


def split_dot(left, right):
    total = None
    rest = left
    for _ in range(3):
        term = rest.astype(jnp.bfloat16)
        rest = rest - term.astype(jnp.float32)
        part = jnp.dot(term, right, preferred_element_type=jnp.float32)
        total = part if total is None else total + part
    return total


def group_sums(columns):
    row = lax.broadcasted_iota(jnp.int32, (columns, LANES), 0)
    col = lax.broadcasted_iota(jnp.int32, (columns, LANES), 1)
    return jnp.where(row // RANK == col, 1.0, 0.0).astype(jnp.bfloat16)


def stage_kernel(cfg, *refs):
    (outer, inner), groups, last, rows = cfg["shape"], cfg["groups"], cfg["last"], cfg["rows"]
    refs = list(refs)

    def take(n):
        return [refs.pop(0) for _ in range(n)]

    x_refs = take(2)
    counts_ref = take(1)[0] if last else None
    pieces = [[take(2) for _ in g["where"]] for g in groups]
    starts = [take(3) if g["carry"] else None for g in groups]
    outs = take(1) if last else None
    totals = [take(3) for _ in groups]
    w, sems = take(2)
    me = lax.axis_index("tok")
    a, b, c = me // (2 * inner), (me // 2) % inner, me % 2
    copies, slot = [], 0
    for g, arrays in zip(groups, pieces):
        for (da, db), pair in zip(g["where"], arrays):
            owner = ((a + outer - da) % outer) * inner + (b + inner - db) % inner
            start = pl.multiple_of(owner * 2 * rows, LANES)
            these = []
            for dc, array in enumerate(pair):
                spot = pl.multiple_of(slot * 2 * rows + ((c + dc) % 2) * rows, LANES)
                these.append((array, w.at[:, pl.ds(spot, rows), :]))
            these = [pltpu.make_async_copy(*ends, sems.at[2 * slot + i]) for i, ends in enumerate(these)]
            for copy in these:
                copy.start()
            copies.append((these, pl.ds(start, 2 * rows)))
            slot += 1
    tiles = w.shape[2] // TILE
    slot = 0
    for g, start, total in zip(groups, starts, totals):
        for first in range(len(g["where"])):
            for copy in copies[slot][0]:
                copy.wait()
            span = slice(slot * 2 * rows, (slot + 1) * 2 * rows)
            came = start if first == 0 else total
            for s in range(2):
                x = x_refs[s][g["layer"], :, copies[slot][1]]
                part = jnp.dot(x, w[s, span, :], preferred_element_type=jnp.float32)
                total[s][...] = part if came is None else came[s][...] + part
            for s in range(2):
                for t in range(tiles):
                    one = w[s, span, t * TILE : (t + 1) * TILE]
                    part = lax.dot_general(one, one, (((0,), (0,)), ((), ())), preferred_element_type=jnp.float32)
                    i = s * tiles + t
                    total[2][i] = part if came is None else came[2][i] + part
            slot += 1
    if last:
        columns = w.shape[2]
        row = lax.broadcasted_iota(jnp.int32, (TILE, TILE), 0)
        col = lax.broadcasted_iota(jnp.int32, (TILE, TILE), 1)
        same = row // RANK == col // RANK
        norm = []
        for t in range(tiles):
            both = sum(total[2][t] * total[2][tiles + t] for total in totals)
            norm.append(jnp.sum(jnp.where(same, both, 0.0), axis=0, keepdims=True))
        norm = jnp.broadcast_to(jnp.concatenate(norm, axis=1), (8, columns))
        chooser = group_sums(columns)
        norm = split_dot(norm, chooser)[:1]
        raw = split_dot(sum(total[0][...] * total[1][...] for total in totals), chooser)
        scaled = raw / jnp.sqrt(norm + 1e-06)
        token = lax.broadcasted_iota(jnp.int32, scaled.shape, 0)
        scaled = jnp.where(token < counts_ref[0], scaled, 0.0)
        outs[0][...] = scaled.T[: columns // RANK]


def stage(shape, groups, gradients, activations, counts=None):
    last = counts is not None
    rows, columns = groups[0]["arrays"][0][0].shape[1:]
    tokens = gradients.shape[1]
    slots = sum(len(g["where"]) for g in groups)
    tiles = 2 * (columns // TILE)
    anywhere = pl.BlockSpec(memory_space=pltpu.HBM)
    vmem = pl.BlockSpec(memory_space=pltpu.VMEM)
    args, specs = [gradients, activations], [vmem, vmem]
    if last:
        args.append(counts)
        specs.append(pl.BlockSpec(memory_space=pltpu.SMEM))
    for g in groups:
        for pair in g["arrays"]:
            args += pair
            specs += [anywhere] * 2
    aliases = {}
    for n, g in enumerate(groups):
        if g["carry"] is not None:
            if not last:
                aliases.update({len(args) + i: 3 * n + i for i in range(3)})
            args += list(g["carry"])
            specs += [vmem] * 3
    sums = [((tokens, columns), jnp.float32)] * 2 + [((tiles, TILE, TILE), jnp.float32)]
    scratch = []
    if last:
        out_shape = jax.ShapeDtypeStruct((columns // RANK, tokens), jnp.float32)
        out_specs = vmem
        scratch = [pltpu.VMEM(*one) for one in sums] * len(groups)
    else:
        out_shape = tuple(jax.ShapeDtypeStruct(*one) for one in sums) * len(groups)
        out_specs = (vmem,) * len(out_shape)
    cfg = dict(
        shape=shape,
        rows=rows,
        last=last,
        groups=[dict(layer=g["layer"], where=g["where"], carry=g["carry"] is not None) for g in groups],
    )
    flops = 4 * slots * rows * columns * (2 * tokens + tiles * TILE)
    return pl.pallas_call(
        functools.partial(stage_kernel, cfg),
        out_shape=out_shape,
        in_specs=specs,
        out_specs=out_specs,
        scratch_shapes=scratch
        + [
            pltpu.VMEM((2, slots * 2 * rows, columns), jnp.bfloat16),
            pltpu.SemaphoreType.DMA((2 * slots,)),
        ],
        input_output_aliases=aliases,
        compiler_params=pltpu.CompilerParams(vmem_limit_bytes=(24 if last else 16) << 20),
        cost_estimate=pl.CostEstimate(
            flops=flops, bytes_accessed=8 * slots * rows * (tokens + columns), transcendentals=0
        ),
    )(*args)


def after(value, *others):
    return lax.optimization_barrier((value,) + others)[0]


def per_device(shape, activations, gradients, query_u, query_v, block_ids, counts):
    outer, inner = shape

    def number(a, b, c):
        return ((a % outer) * inner + b % inner) * 2 + c % 2

    def move(value, da, db, dc):
        steps = [
            (number(a, b, c), number(a + da, b + db, c + dc))
            for a in range(outer)
            for b in range(inner)
            for c in range(2)
        ]
        return lax.ppermute(value, "tok", steps)

    have, pairs = [{}, {}], [{}, {}]
    for layer in range(2):
        have[layer][(0, 0)] = pick(layer, query_u, query_v, block_ids)
    for da in range(outer):
        for layer in range(2):
            h = have[layer]
            if da < outer - 1:
                fed = h[(da, 0)]
                if da:
                    fed = after(fed, h[(da - 1, 1)])
                h[(da + 1, 0)] = move(fed, 1, 0, 0)
            if da == outer - 1 and layer == 1:
                fed = after(h[(0, 1)], h[(da, 0)])
                h[(da, 1)] = move(fed, -1, 0, 0)
            else:
                h[(da, 1)] = move(h[(da, 0)], 0, 1, 0)
    for layer in range(2):
        for key, piece in have[layer].items():
            pairs[layer][key] = [piece, move(piece, 0, 0, 1)]

    gradients, activations = load(gradients, activations)

    def group(layer, keys, carry):
        return dict(layer=layer, where=keys, arrays=[pairs[layer][key] for key in keys], carry=carry)

    parts = [[(0, 0), (0, 1), (1, 0)]] + [[(da, 1), (da + 1, 0)] for da in range(1, outer - 1)]
    carry = [None, None]
    for keys in parts:
        for layer in range(2):
            carry[layer] = stage(shape, [group(layer, keys, carry[layer])], gradients, activations)
    scores = stage(
        shape,
        [group(layer, [(outer - 1, 1)], carry[layer]) for layer in range(2)],
        gradients,
        activations,
        counts=counts,
    )
    return scores.T


def solution(mesh):
    spec = (
        P(None, ("groups", "tok"), None),
        P(None, ("groups", "tok"), None),
        P("groups", "tok", None),
        P("groups", "tok", None),
        P("groups", None),
        P(("groups", "tok")),
    )
    members = mesh.shape["tok"]
    shape = (OUTER, members // (2 * OUTER))
    ring = members == 4 * OUTER

    def body(*args):
        fits = ring and args[2].shape[1] % LANES == 0
        return per_device(shape, *args) if fits else per_device_plain(*args)

    return jax.shard_map(body, mesh=mesh, in_specs=spec, out_specs=P(("groups", "tok"), None), check_vma=False)
```

```python
import functools

import jax
import jax.numpy as jnp
from jax import lax
from jax.experimental import pallas as pl
from jax.experimental.pallas import tpu as pltpu
from jax.sharding import PartitionSpec as P


RANK = 8
QB = 4
OUTER = 4
LANES = 128
TILE = 256


def pick_columns(factor, block_ids):
    width = QB * RANK
    chosen = []
    for layer in range(factor.shape[0]):
        slots = factor[layer].reshape(factor.shape[1], -1, width)
        chosen.append(jnp.take(slots, block_ids[layer], axis=1).reshape(factor.shape[1], -1))
    return jnp.stack(chosen)


def rank_grams(factor):
    per = factor.reshape(factor.shape[0], factor.shape[1], -1, RANK)
    return jnp.einsum("lkqr,lkqs->lqrs", per, per, preferred_element_type=jnp.float32)


def per_device_plain(activations, gradients, query_u, query_v, block_ids, counts):
    layers, tok_rows, _ = activations.shape
    columns = block_ids.shape[1] * QB * RANK
    queries = columns // RANK
    whole_u = lax.all_gather(pick_columns(query_u, block_ids), "tok", axis=1, tiled=True)
    whole_v = lax.all_gather(pick_columns(query_v, block_ids), "tok", axis=1, tiled=True)
    grad_proj = jnp.einsum("ltk,lkc->ltc", gradients, whole_u, preferred_element_type=jnp.float32)
    act_proj = jnp.einsum("ltk,lkc->ltc", activations, whole_v, preferred_element_type=jnp.float32)
    raw = jnp.sum((grad_proj * act_proj).reshape(layers, tok_rows, queries, RANK), axis=(0, 3))
    norm_sq = jnp.sum(rank_grams(whole_u) * rank_grams(whole_v), axis=(0, 2, 3))
    live = jnp.arange(tok_rows, dtype=jnp.int32) < counts[0]
    scaled = raw / jnp.sqrt(norm_sq + 1e-06)[None, :]
    return jnp.where(live[:, None], scaled, jnp.zeros_like(scaled))


def pick_kernel(layer, ids_hbm, u_ref, v_ref, out_ref, ids_ref, held, made, sems):
    width = QB * RANK
    rows = u_ref.shape[1]
    columns = out_ref.shape[2]
    per = LANES // width
    named = pltpu.make_async_copy(ids_hbm, ids_ref, sems.at[4])
    named.start()
    copies = [
        pltpu.make_async_copy(ref.at[layer], held.at[s], sems.at[s]) for s, ref in enumerate((u_ref, v_ref))
    ]
    for copy in copies:
        copy.start()
    named.wait()
    lane = lax.broadcasted_iota(jnp.int32, (rows, LANES), 1) // width
    outs = []
    for s in range(2):
        copies[s].wait()
        for chunk in range(columns // LANES):
            total = None
            for k in range(per):
                stored = ids_ref[layer, chunk * per + k]
                start = pl.multiple_of((stored // per) * LANES, LANES)
                part = held[s, :, pl.ds(start, LANES)].astype(jnp.float32)
                part = pltpu.roll(part, lax.rem(k - stored % per + per, per) * width, 1)
                total = part if total is None else jnp.where(lane == k, part, total)
            made[s, :, chunk * LANES : (chunk + 1) * LANES] = total.astype(jnp.bfloat16)
        out = pltpu.make_async_copy(made.at[s], out_ref.at[s], sems.at[2 + s])
        out.start()
        outs.append(out)
    for out in outs:
        out.wait()


def pick(layer, query_u, query_v, block_ids):
    _, rows, bank = query_u.shape
    columns = block_ids.shape[1] * QB * RANK
    anywhere = pl.BlockSpec(memory_space=pltpu.HBM)
    return pl.pallas_call(
        functools.partial(pick_kernel, layer),
        out_shape=jax.ShapeDtypeStruct((2, rows, columns), jnp.bfloat16),
        in_specs=[anywhere] * 3,
        out_specs=anywhere,
        scratch_shapes=[
            pltpu.SMEM(block_ids.shape, jnp.int32),
            pltpu.VMEM((2, rows, bank), jnp.bfloat16),
            pltpu.VMEM((2, rows, columns), jnp.bfloat16),
            pltpu.SemaphoreType.DMA((5,)),
        ],
        cost_estimate=pl.CostEstimate(
            flops=4 * rows * columns, bytes_accessed=4 * rows * (bank + columns), transcendentals=0
        ),
    )(block_ids, query_u, query_v)


def load_kernel(*refs):
    half = len(refs) // 2
    sems = refs[-1]
    copies = [pltpu.make_async_copy(refs[i], refs[half + i], sems.at[i]) for i in range(half)]
    for copy in copies:
        copy.start()
    for copy in copies:
        copy.wait()


def load(*arrays):
    return pl.pallas_call(
        load_kernel,
        out_shape=tuple(jax.ShapeDtypeStruct(one.shape, one.dtype) for one in arrays),
        in_specs=[pl.BlockSpec(memory_space=pltpu.HBM)] * len(arrays),
        out_specs=(pl.BlockSpec(memory_space=pltpu.VMEM),) * len(arrays),
        scratch_shapes=[pltpu.SemaphoreType.DMA((len(arrays),))],
        compiler_params=pltpu.CompilerParams(vmem_limit_bytes=42 << 20),
        name="load",
    )(*arrays)


def split_dot(left, right):
    total = None
    rest = left
    for _ in range(3):
        term = rest.astype(jnp.bfloat16)
        rest = rest - term.astype(jnp.float32)
        part = jnp.dot(term, right, preferred_element_type=jnp.float32)
        total = part if total is None else total + part
    return total


def group_sums(columns):
    row = lax.broadcasted_iota(jnp.int32, (columns, LANES), 0)
    col = lax.broadcasted_iota(jnp.int32, (columns, LANES), 1)
    return jnp.where(row // RANK == col, 1.0, 0.0).astype(jnp.bfloat16)


def stage_kernel(cfg, *refs):
    (outer, inner), groups, last, rows = cfg["shape"], cfg["groups"], cfg["last"], cfg["rows"]
    refs = list(refs)

    def take(n):
        return [refs.pop(0) for _ in range(n)]

    x_refs = take(2)
    counts_hbm = take(1)[0] if last else None
    pieces = [[take(2) for _ in g["where"]] for g in groups]
    starts = [take(3) if g["carry"] else None for g in groups]
    outs = take(1) if last else None
    product, counts_ref = take(2) if last else (None, None)
    totals = [take(3) for _ in groups]
    w, sems = take(2)
    me = lax.axis_index("tok")
    a, b, c = me // (2 * inner), (me // 2) % inner, me % 2
    copies, slot = [], 0
    for g, arrays in zip(groups, pieces):
        for (da, db), pair in zip(g["where"], arrays):
            owner = ((a + outer - da) % outer) * inner + (b + inner - db) % inner
            start = pl.multiple_of(owner * 2 * rows, LANES)
            these = []
            for dc, array in enumerate(pair):
                spot = pl.multiple_of(slot * 2 * rows + ((c + dc) % 2) * rows, LANES)
                these.append((array, w.at[:, pl.ds(spot, rows), :]))
            these = [pltpu.make_async_copy(*ends, sems.at[2 * slot + i]) for i, ends in enumerate(these)]
            for copy in these:
                copy.start()
            copies.append((these, pl.ds(start, 2 * rows)))
            slot += 1
    if last:
        live = pltpu.make_async_copy(counts_hbm, counts_ref, sems.at[2 * slot])
        live.start()
    tiles = w.shape[2] // TILE
    slot = 0
    for g, start, total in zip(groups, starts, totals):
        for first in range(len(g["where"])):
            for copy in copies[slot][0]:
                copy.wait()
            span = slice(slot * 2 * rows, (slot + 1) * 2 * rows)
            came = start if first == 0 else total
            for s in range(2):
                x = x_refs[s][g["layer"], :, copies[slot][1]]
                part = jnp.dot(x, w[s, span, :], preferred_element_type=jnp.float32)
                if came is not None:
                    part = came[s][...] + part
                if last and s == 1:
                    part = total[0][...] * part
                    product[...] = part if g is groups[0] else product[...] + part
                else:
                    total[s][...] = part
            for s in range(2):
                for t in range(tiles):
                    one = w[s, span, t * TILE : (t + 1) * TILE]
                    part = lax.dot_general(one, one, (((0,), (0,)), ((), ())), preferred_element_type=jnp.float32)
                    i = s * tiles + t
                    total[2][i] = part if came is None else came[2][i] + part
            slot += 1
    if last:
        columns = w.shape[2]
        row = lax.broadcasted_iota(jnp.int32, (TILE, TILE), 0)
        col = lax.broadcasted_iota(jnp.int32, (TILE, TILE), 1)
        same = row // RANK == col // RANK
        norm = []
        for t in range(tiles):
            both = sum(total[2][t] * total[2][tiles + t] for total in totals)
            norm.append(jnp.sum(jnp.where(same, both, 0.0), axis=0, keepdims=True))
        norm = jnp.broadcast_to(jnp.concatenate(norm, axis=1), (8, columns))
        chooser = group_sums(columns)
        norm = split_dot(norm, chooser)[:1]
        raw = split_dot(product[...], chooser)
        scaled = raw / jnp.sqrt(norm + 1e-06)
        live.wait()
        token = lax.broadcasted_iota(jnp.int32, scaled.shape, 0)
        scaled = jnp.where(token < counts_ref[0], scaled, 0.0)
        outs[0][...] = scaled.T[: columns // RANK]


def stage(shape, groups, gradients, activations, counts=None):
    last = counts is not None
    rows, columns = groups[0]["arrays"][0][0].shape[1:]
    tokens = gradients.shape[1]
    slots = sum(len(g["where"]) for g in groups)
    tiles = 2 * (columns // TILE)
    anywhere = pl.BlockSpec(memory_space=pltpu.HBM)
    vmem = pl.BlockSpec(memory_space=pltpu.VMEM)
    args, specs = [gradients, activations], [vmem, vmem]
    if last:
        args.append(counts)
        specs.append(anywhere)
    for g in groups:
        for pair in g["arrays"]:
            args += pair
            specs += [anywhere] * 2
    aliases = {}
    for n, g in enumerate(groups):
        if g["carry"] is not None:
            if not last:
                aliases.update({len(args) + i: 3 * n + i for i in range(3)})
            args += list(g["carry"])
            specs += [vmem] * 3
    sums = [((tokens, columns), jnp.float32)] * 2 + [((tiles, TILE, TILE), jnp.float32)]
    scratch = []
    if last:
        out_shape = jax.ShapeDtypeStruct((columns // RANK, tokens), jnp.float32)
        out_specs = vmem
        scratch = [pltpu.VMEM(*sums[0]), pltpu.SMEM(counts.shape, jnp.int32)] + [pltpu.VMEM(*one) for one in sums] * len(groups)
    else:
        out_shape = tuple(jax.ShapeDtypeStruct(*one) for one in sums) * len(groups)
        out_specs = (vmem,) * len(out_shape)
    cfg = dict(
        shape=shape,
        rows=rows,
        last=last,
        groups=[dict(layer=g["layer"], where=g["where"], carry=g["carry"] is not None) for g in groups],
    )
    flops = 4 * slots * rows * columns * (2 * tokens + tiles * TILE)
    return pl.pallas_call(
        functools.partial(stage_kernel, cfg),
        out_shape=out_shape,
        in_specs=specs,
        out_specs=out_specs,
        scratch_shapes=scratch
        + [
            pltpu.VMEM((2, slots * 2 * rows, columns), jnp.bfloat16),
            pltpu.SemaphoreType.DMA((2 * slots + 1,)),
        ],
        input_output_aliases=aliases,
        compiler_params=pltpu.CompilerParams(vmem_limit_bytes=(24 if last else 16) << 20),
        cost_estimate=pl.CostEstimate(
            flops=flops, bytes_accessed=8 * slots * rows * (tokens + columns), transcendentals=0
        ),
    )(*args)


def after(value, *others):
    return lax.optimization_barrier((value,) + others)[0]


def per_device(shape, activations, gradients, query_u, query_v, block_ids, counts):
    outer, inner = shape

    def number(a, b, c):
        return ((a % outer) * inner + b % inner) * 2 + c % 2

    def move(value, da, db, dc):
        steps = [
            (number(a, b, c), number(a + da, b + db, c + dc))
            for a in range(outer)
            for b in range(inner)
            for c in range(2)
        ]
        return lax.ppermute(value, "tok", steps)

    have, pairs = [{}, {}], [{}, {}]
    for layer in range(2):
        have[layer][(0, 0)] = pick(layer, query_u, query_v, block_ids)
    for da in range(outer):
        for layer in range(2):
            h = have[layer]
            if da < outer - 1:
                fed = h[(da, 0)]
                if da:
                    fed = after(fed, h[(da - 1, 1)])
                h[(da + 1, 0)] = move(fed, 1, 0, 0)
            if da == outer - 1 and layer == 1:
                fed = after(h[(0, 1)], h[(da, 0)])
                h[(da, 1)] = move(fed, -1, 0, 0)
            else:
                h[(da, 1)] = move(h[(da, 0)], 0, 1, 0)
    for layer in range(2):
        for key, piece in have[layer].items():
            pairs[layer][key] = [piece, move(piece, 0, 0, 1)]

    gradients, activations = load(gradients, activations)

    def group(layer, keys, carry):
        return dict(layer=layer, where=keys, arrays=[pairs[layer][key] for key in keys], carry=carry)

    parts = [[(0, 0), (0, 1), (1, 0)]] + [[(da, 1), (da + 1, 0)] for da in range(1, outer - 1)]
    carry = [None, None]
    for keys in parts:
        for layer in range(2):
            carry[layer] = stage(shape, [group(layer, keys, carry[layer])], gradients, activations)
    scores = stage(
        shape,
        [group(layer, [(outer - 1, 1)], carry[layer]) for layer in range(2)],
        gradients,
        activations,
        counts=counts,
    )
    return scores.T


def solution(mesh):
    spec = (
        P(None, ("groups", "tok"), None),
        P(None, ("groups", "tok"), None),
        P("groups", "tok", None),
        P("groups", "tok", None),
        P("groups", None),
        P(("groups", "tok")),
    )
    members = mesh.shape["tok"]
    shape = (OUTER, members // (2 * OUTER))
    ring = members == 4 * OUTER

    def body(*args):
        fits = ring and args[2].shape[1] % LANES == 0
        return per_device(shape, *args) if fits else per_device_plain(*args)

    return jax.shard_map(body, mesh=mesh, in_specs=spec, out_specs=P(("groups", "tok"), None), check_vma=False)
```

```python
import functools

import jax
import jax.numpy as jnp
from jax import lax
from jax.experimental import pallas as pl
from jax.experimental.pallas import tpu as pltpu
from jax.sharding import PartitionSpec as P


RANK = 8
QB = 4
OUTER = 4
LANES = 128
TILE = 256


def pick_columns(factor, block_ids):
    width = QB * RANK
    chosen = []
    for layer in range(factor.shape[0]):
        slots = factor[layer].reshape(factor.shape[1], -1, width)
        chosen.append(jnp.take(slots, block_ids[layer], axis=1).reshape(factor.shape[1], -1))
    return jnp.stack(chosen)


def rank_grams(factor):
    per = factor.reshape(factor.shape[0], factor.shape[1], -1, RANK)
    return jnp.einsum("lkqr,lkqs->lqrs", per, per, preferred_element_type=jnp.float32)


def per_device_plain(activations, gradients, query_u, query_v, block_ids, counts):
    layers, tok_rows, _ = activations.shape
    columns = block_ids.shape[1] * QB * RANK
    queries = columns // RANK
    whole_u = lax.all_gather(pick_columns(query_u, block_ids), "tok", axis=1, tiled=True)
    whole_v = lax.all_gather(pick_columns(query_v, block_ids), "tok", axis=1, tiled=True)
    grad_proj = jnp.einsum("ltk,lkc->ltc", gradients, whole_u, preferred_element_type=jnp.float32)
    act_proj = jnp.einsum("ltk,lkc->ltc", activations, whole_v, preferred_element_type=jnp.float32)
    raw = jnp.sum((grad_proj * act_proj).reshape(layers, tok_rows, queries, RANK), axis=(0, 3))
    norm_sq = jnp.sum(rank_grams(whole_u) * rank_grams(whole_v), axis=(0, 2, 3))
    live = jnp.arange(tok_rows, dtype=jnp.int32) < counts[0]
    scaled = raw / jnp.sqrt(norm_sq + 1e-06)[None, :]
    return jnp.where(live[:, None], scaled, jnp.zeros_like(scaled))


def pick_kernel(layer, ids_hbm, u_ref, v_ref, out_ref, ids_ref, held, made, sems):
    width = QB * RANK
    rows = u_ref.shape[1]
    columns = out_ref.shape[2]
    per = LANES // width
    named = pltpu.make_async_copy(ids_hbm, ids_ref, sems.at[4])
    named.start()
    copies = [
        pltpu.make_async_copy(ref.at[layer], held.at[s], sems.at[s]) for s, ref in enumerate((u_ref, v_ref))
    ]
    for copy in copies:
        copy.start()
    named.wait()
    lane = lax.broadcasted_iota(jnp.int32, (rows, LANES), 1) // width
    outs = []
    for s in range(2):
        copies[s].wait()
        for chunk in range(columns // LANES):
            total = None
            for k in range(per):
                stored = ids_ref[layer, chunk * per + k]
                start = pl.multiple_of((stored // per) * LANES, LANES)
                part = held[s, :, pl.ds(start, LANES)].astype(jnp.float32)
                part = pltpu.roll(part, lax.rem(k - stored % per + per, per) * width, 1)
                total = part if total is None else jnp.where(lane == k, part, total)
            made[s, :, chunk * LANES : (chunk + 1) * LANES] = total.astype(jnp.bfloat16)
        out = pltpu.make_async_copy(made.at[s], out_ref.at[s], sems.at[2 + s])
        out.start()
        outs.append(out)
    for out in outs:
        out.wait()


def pick(layer, query_u, query_v, block_ids):
    _, rows, bank = query_u.shape
    columns = block_ids.shape[1] * QB * RANK
    anywhere = pl.BlockSpec(memory_space=pltpu.HBM)
    return pl.pallas_call(
        functools.partial(pick_kernel, layer),
        out_shape=jax.ShapeDtypeStruct((2, rows, columns), jnp.bfloat16),
        in_specs=[anywhere] * 3,
        out_specs=anywhere,
        scratch_shapes=[
            pltpu.SMEM(block_ids.shape, jnp.int32),
            pltpu.VMEM((2, rows, bank), jnp.bfloat16),
            pltpu.VMEM((2, rows, columns), jnp.bfloat16),
            pltpu.SemaphoreType.DMA((5,)),
        ],
        cost_estimate=pl.CostEstimate(
            flops=4 * rows * columns, bytes_accessed=4 * rows * (bank + columns), transcendentals=0
        ),
    )(block_ids, query_u, query_v)


def load_kernel(counts_ref, *refs):
    half = (len(refs) - 1) // 2
    sems = refs[-1]
    live_ref = refs[half]
    copies = [pltpu.make_async_copy(refs[i], refs[half + 1 + i], sems.at[i]) for i in range(half)]
    for copy in copies:
        copy.start()
    live_ref[...] = jnp.full(live_ref.shape, counts_ref[0], jnp.int32)
    for copy in copies:
        copy.wait()


def load(counts, *arrays):
    outs = [jax.ShapeDtypeStruct((8, LANES), jnp.int32)]
    outs += [jax.ShapeDtypeStruct(one.shape, one.dtype) for one in arrays]
    return pl.pallas_call(
        load_kernel,
        out_shape=tuple(outs),
        in_specs=[pl.BlockSpec(memory_space=pltpu.SMEM)]
        + [pl.BlockSpec(memory_space=pltpu.HBM)] * len(arrays),
        out_specs=(pl.BlockSpec(memory_space=pltpu.VMEM),) * len(outs),
        scratch_shapes=[pltpu.SemaphoreType.DMA((len(arrays),))],
        compiler_params=pltpu.CompilerParams(vmem_limit_bytes=42 << 20),
        name="load",
    )(counts, *arrays)


def split_dot(left, right):
    total = None
    rest = left
    for _ in range(3):
        term = rest.astype(jnp.bfloat16)
        rest = rest - term.astype(jnp.float32)
        part = jnp.dot(term, right, preferred_element_type=jnp.float32)
        total = part if total is None else total + part
    return total


def group_sums(columns):
    row = lax.broadcasted_iota(jnp.int32, (columns, LANES), 0)
    col = lax.broadcasted_iota(jnp.int32, (columns, LANES), 1)
    return jnp.where(row // RANK == col, 1.0, 0.0).astype(jnp.bfloat16)


def stage_kernel(cfg, *refs):
    (outer, inner), groups, last, rows = cfg["shape"], cfg["groups"], cfg["last"], cfg["rows"]
    refs = list(refs)

    def take(n):
        return [refs.pop(0) for _ in range(n)]

    x_refs = take(2)
    live_ref = take(1)[0] if last else None
    pieces = [[take(2) for _ in g["where"]] for g in groups]
    starts = [take(3) if g["carry"] else None for g in groups]
    outs = take(1) if last else None
    product = take(1)[0] if last else None
    totals = [take(3) for _ in groups]
    w, sems = take(2)
    me = lax.axis_index("tok")
    a, b, c = me // (2 * inner), (me // 2) % inner, me % 2
    copies, slot = [], 0
    for g, arrays in zip(groups, pieces):
        for (da, db), pair in zip(g["where"], arrays):
            owner = ((a + outer - da) % outer) * inner + (b + inner - db) % inner
            start = pl.multiple_of(owner * 2 * rows, LANES)
            these = []
            for dc, array in enumerate(pair):
                spot = pl.multiple_of(slot * 2 * rows + ((c + dc) % 2) * rows, LANES)
                these.append((array, w.at[:, pl.ds(spot, rows), :]))
            these = [pltpu.make_async_copy(*ends, sems.at[2 * slot + i]) for i, ends in enumerate(these)]
            for copy in these:
                copy.start()
            copies.append((these, pl.ds(start, 2 * rows)))
            slot += 1
    tiles = w.shape[2] // TILE
    slot = 0
    for g, start, total in zip(groups, starts, totals):
        for first in range(len(g["where"])):
            for copy in copies[slot][0]:
                copy.wait()
            span = slice(slot * 2 * rows, (slot + 1) * 2 * rows)
            came = start if first == 0 else total
            for s in range(2):
                x = x_refs[s][g["layer"], :, copies[slot][1]]
                part = jnp.dot(x, w[s, span, :], preferred_element_type=jnp.float32)
                if came is not None:
                    part = came[s][...] + part
                if last and s == 1:
                    part = total[0][...] * part
                    product[...] = part if g is groups[0] else product[...] + part
                else:
                    total[s][...] = part
            for s in range(2):
                for t in range(tiles):
                    one = w[s, span, t * TILE : (t + 1) * TILE]
                    part = lax.dot_general(one, one, (((0,), (0,)), ((), ())), preferred_element_type=jnp.float32)
                    i = s * tiles + t
                    total[2][i] = part if came is None else came[2][i] + part
            slot += 1
    if last:
        columns = w.shape[2]
        row = lax.broadcasted_iota(jnp.int32, (TILE, TILE), 0)
        col = lax.broadcasted_iota(jnp.int32, (TILE, TILE), 1)
        same = row // RANK == col // RANK
        norm = []
        for t in range(tiles):
            both = sum(total[2][t] * total[2][tiles + t] for total in totals)
            norm.append(jnp.sum(jnp.where(same, both, 0.0), axis=0, keepdims=True))
        norm = jnp.broadcast_to(jnp.concatenate(norm, axis=1), (8, columns))
        chooser = group_sums(columns)
        norm = split_dot(norm, chooser)[:1]
        raw = split_dot(product[...], chooser)
        scaled = raw / jnp.sqrt(norm + 1e-06)
        token = lax.broadcasted_iota(jnp.int32, scaled.shape, 0)
        scaled = jnp.where(token < live_ref[:1], scaled, 0.0)
        outs[0][...] = scaled.T[: columns // RANK]


def stage(shape, groups, gradients, activations, live=None):
    last = live is not None
    rows, columns = groups[0]["arrays"][0][0].shape[1:]
    tokens = gradients.shape[1]
    slots = sum(len(g["where"]) for g in groups)
    tiles = 2 * (columns // TILE)
    anywhere = pl.BlockSpec(memory_space=pltpu.HBM)
    vmem = pl.BlockSpec(memory_space=pltpu.VMEM)
    args, specs = [gradients, activations], [vmem, vmem]
    if last:
        args.append(live)
        specs.append(vmem)
    for g in groups:
        for pair in g["arrays"]:
            args += pair
            specs += [anywhere] * 2
    aliases = {}
    for n, g in enumerate(groups):
        if g["carry"] is not None:
            if not last:
                aliases.update({len(args) + i: 3 * n + i for i in range(3)})
            args += list(g["carry"])
            specs += [vmem] * 3
    sums = [((tokens, columns), jnp.float32)] * 2 + [((tiles, TILE, TILE), jnp.float32)]
    scratch = []
    if last:
        out_shape = jax.ShapeDtypeStruct((columns // RANK, tokens), jnp.float32)
        out_specs = vmem
        scratch = [pltpu.VMEM(*sums[0])] + [pltpu.VMEM(*one) for one in sums] * len(groups)
    else:
        out_shape = tuple(jax.ShapeDtypeStruct(*one) for one in sums) * len(groups)
        out_specs = (vmem,) * len(out_shape)
    cfg = dict(
        shape=shape,
        rows=rows,
        last=last,
        groups=[dict(layer=g["layer"], where=g["where"], carry=g["carry"] is not None) for g in groups],
    )
    flops = 4 * slots * rows * columns * (2 * tokens + tiles * TILE)
    return pl.pallas_call(
        functools.partial(stage_kernel, cfg),
        out_shape=out_shape,
        in_specs=specs,
        out_specs=out_specs,
        scratch_shapes=scratch
        + [
            pltpu.VMEM((2, slots * 2 * rows, columns), jnp.bfloat16),
            pltpu.SemaphoreType.DMA((2 * slots,)),
        ],
        input_output_aliases=aliases,
        compiler_params=pltpu.CompilerParams(vmem_limit_bytes=(24 if last else 16) << 20),
        cost_estimate=pl.CostEstimate(
            flops=flops, bytes_accessed=8 * slots * rows * (tokens + columns), transcendentals=0
        ),
    )(*args)


def after(value, *others):
    return lax.optimization_barrier((value,) + others)[0]


def per_device(shape, activations, gradients, query_u, query_v, block_ids, counts):
    outer, inner = shape

    def number(a, b, c):
        return ((a % outer) * inner + b % inner) * 2 + c % 2

    def move(value, da, db, dc):
        steps = [
            (number(a, b, c), number(a + da, b + db, c + dc))
            for a in range(outer)
            for b in range(inner)
            for c in range(2)
        ]
        return lax.ppermute(value, "tok", steps)

    have, pairs = [{}, {}], [{}, {}]
    for layer in range(2):
        have[layer][(0, 0)] = pick(layer, query_u, query_v, block_ids)
    for da in range(outer):
        for layer in range(2):
            h = have[layer]
            if da < outer - 1:
                fed = h[(da, 0)]
                if da:
                    fed = after(fed, h[(da - 1, 1)])
                h[(da + 1, 0)] = move(fed, 1, 0, 0)
            if da == outer - 1 and layer == 1:
                fed = after(h[(0, 1)], have[0][(da, 0)])
                h[(da, 1)] = move(fed, -1, 0, 0)
            else:
                h[(da, 1)] = move(h[(da, 0)], 0, 1, 0)
    for layer in range(2):
        for key, piece in have[layer].items():
            pairs[layer][key] = [piece, move(piece, 0, 0, 1)]

    live, gradients, activations = load(counts, gradients, activations)

    def group(layer, keys, carry):
        return dict(layer=layer, where=keys, arrays=[pairs[layer][key] for key in keys], carry=carry)

    parts = [[(0, 0), (0, 1), (1, 0)]] + [[(da, 1), (da + 1, 0)] for da in range(1, outer - 1)]
    carry = [None, None]
    for keys in parts:
        for layer in range(2):
            carry[layer] = stage(shape, [group(layer, keys, carry[layer])], gradients, activations)
    scores = stage(
        shape, [group(layer, [(outer - 1, 1)], carry[layer]) for layer in range(2)], gradients, activations, live=live
    )
    return scores.T


def solution(mesh):
    spec = (
        P(None, ("groups", "tok"), None),
        P(None, ("groups", "tok"), None),
        P("groups", "tok", None),
        P("groups", "tok", None),
        P("groups", None),
        P(("groups", "tok")),
    )
    members = mesh.shape["tok"]
    shape = (OUTER, members // (2 * OUTER))
    ring = members == 4 * OUTER

    def body(*args):
        fits = ring and args[2].shape[1] % LANES == 0
        return per_device(shape, *args) if fits else per_device_plain(*args)

    return jax.shard_map(body, mesh=mesh, in_specs=spec, out_specs=P(("groups", "tok"), None), check_vma=False)
```

```python
import functools

import jax
import jax.numpy as jnp
from jax import lax
from jax.experimental import pallas as pl
from jax.experimental.pallas import tpu as pltpu
from jax.sharding import PartitionSpec as P


RANK = 8
QB = 4
OUTER = 4
LANES = 128
TILE = 256
LOAD_GRANTS = (46 << 20, 45 << 20)


def pick_columns(factor, block_ids):
    width = QB * RANK
    chosen = []
    for layer in range(factor.shape[0]):
        slots = factor[layer].reshape(factor.shape[1], -1, width)
        chosen.append(jnp.take(slots, block_ids[layer], axis=1).reshape(factor.shape[1], -1))
    return jnp.stack(chosen)


def rank_grams(factor):
    per = factor.reshape(factor.shape[0], factor.shape[1], -1, RANK)
    return jnp.einsum("lkqr,lkqs->lqrs", per, per, preferred_element_type=jnp.float32)


def per_device_plain(activations, gradients, query_u, query_v, block_ids, counts):
    layers, tok_rows, _ = activations.shape
    columns = block_ids.shape[1] * QB * RANK
    queries = columns // RANK
    whole_u = lax.all_gather(pick_columns(query_u, block_ids), "tok", axis=1, tiled=True)
    whole_v = lax.all_gather(pick_columns(query_v, block_ids), "tok", axis=1, tiled=True)
    grad_proj = jnp.einsum("ltk,lkc->ltc", gradients, whole_u, preferred_element_type=jnp.float32)
    act_proj = jnp.einsum("ltk,lkc->ltc", activations, whole_v, preferred_element_type=jnp.float32)
    raw = jnp.sum((grad_proj * act_proj).reshape(layers, tok_rows, queries, RANK), axis=(0, 3))
    norm_sq = jnp.sum(rank_grams(whole_u) * rank_grams(whole_v), axis=(0, 2, 3))
    live = jnp.arange(tok_rows, dtype=jnp.int32) < counts[0]
    scaled = raw / jnp.sqrt(norm_sq + 1e-06)[None, :]
    return jnp.where(live[:, None], scaled, jnp.zeros_like(scaled))


def pick_kernel(layer, ids_hbm, u_ref, v_ref, out_ref, ids_ref, held, made, sems):
    width = QB * RANK
    rows = u_ref.shape[1]
    columns = out_ref.shape[2]
    per = LANES // width
    named = pltpu.make_async_copy(ids_hbm, ids_ref, sems.at[4])
    named.start()
    copies = [
        pltpu.make_async_copy(ref.at[layer], held.at[s], sems.at[s]) for s, ref in enumerate((u_ref, v_ref))
    ]
    for copy in copies:
        copy.start()
    named.wait()
    lane = lax.broadcasted_iota(jnp.int32, (rows, LANES), 1) // width
    outs = []
    for s in range(2):
        copies[s].wait()
        for chunk in range(columns // LANES):
            total = None
            for k in range(per):
                stored = ids_ref[layer, chunk * per + k]
                start = pl.multiple_of((stored // per) * LANES, LANES)
                part = held[s, :, pl.ds(start, LANES)].astype(jnp.float32)
                part = pltpu.roll(part, lax.rem(k - stored % per + per, per) * width, 1)
                total = part if total is None else jnp.where(lane == k, part, total)
            made[s, :, chunk * LANES : (chunk + 1) * LANES] = total.astype(jnp.bfloat16)
        out = pltpu.make_async_copy(made.at[s], out_ref.at[s], sems.at[2 + s])
        out.start()
        outs.append(out)
    for out in outs:
        out.wait()


def pick(layer, query_u, query_v, block_ids):
    _, rows, bank = query_u.shape
    columns = block_ids.shape[1] * QB * RANK
    anywhere = pl.BlockSpec(memory_space=pltpu.HBM)
    return pl.pallas_call(
        functools.partial(pick_kernel, layer),
        out_shape=jax.ShapeDtypeStruct((2, rows, columns), jnp.bfloat16),
        in_specs=[anywhere] * 3,
        out_specs=anywhere,
        scratch_shapes=[
            pltpu.SMEM(block_ids.shape, jnp.int32),
            pltpu.VMEM((2, rows, bank), jnp.bfloat16),
            pltpu.VMEM((2, rows, columns), jnp.bfloat16),
            pltpu.SemaphoreType.DMA((5,)),
        ],
        cost_estimate=pl.CostEstimate(
            flops=4 * rows * columns, bytes_accessed=4 * rows * (bank + columns), transcendentals=0
        ),
    )(block_ids, query_u, query_v)


def load_kernel(layer, *refs):
    half = (len(refs) - 2) // 2 if layer == 0 else (len(refs) - 1) // 2
    refs, sems = list(refs[:-1]), refs[-1]
    if layer == 0:
        counts_ref, live_ref = refs.pop(0), refs.pop(half)
    copies = [pltpu.make_async_copy(refs[i].at[layer], refs[half + i], sems.at[i]) for i in range(half)]
    for copy in copies:
        copy.start()
    if layer == 0:
        live_ref[...] = jnp.full(live_ref.shape, counts_ref[0], jnp.int32)
    for copy in copies:
        copy.wait()


def load(layer, counts, *arrays):
    outs = [jax.ShapeDtypeStruct((8, LANES), jnp.int32)] if layer == 0 else []
    outs += [jax.ShapeDtypeStruct(one.shape[1:], one.dtype) for one in arrays]
    specs = [pl.BlockSpec(memory_space=pltpu.SMEM)] if layer == 0 else []
    args = ([counts] if layer == 0 else []) + list(arrays)
    return pl.pallas_call(
        functools.partial(load_kernel, layer),
        out_shape=tuple(outs),
        in_specs=specs + [pl.BlockSpec(memory_space=pltpu.HBM)] * len(arrays),
        out_specs=(pl.BlockSpec(memory_space=pltpu.VMEM),) * len(outs),
        scratch_shapes=[pltpu.SemaphoreType.DMA((len(arrays),))],
        compiler_params=pltpu.CompilerParams(vmem_limit_bytes=LOAD_GRANTS[layer]),
    )(*args)


def split_dot(left, right):
    total = None
    rest = left
    for _ in range(3):
        term = rest.astype(jnp.bfloat16)
        rest = rest - term.astype(jnp.float32)
        part = jnp.dot(term, right, preferred_element_type=jnp.float32)
        total = part if total is None else total + part
    return total


def group_sums(columns):
    row = lax.broadcasted_iota(jnp.int32, (columns, LANES), 0)
    col = lax.broadcasted_iota(jnp.int32, (columns, LANES), 1)
    return jnp.where(row // RANK == col, 1.0, 0.0).astype(jnp.bfloat16)


def stage_kernel(cfg, *refs):
    (outer, inner), groups, last, rows = cfg["shape"], cfg["groups"], cfg["last"], cfg["rows"]
    refs = list(refs)

    def take(n):
        return [refs.pop(0) for _ in range(n)]

    x_refs = [take(2) for _ in groups]
    live_ref = take(1)[0] if last else None
    pieces = [[take(2) for _ in g["where"]] for g in groups]
    starts = [take(3) if g["carry"] else None for g in groups]
    outs = take(1) if last else None
    product, made = take(2) if last else (None, None)
    totals = [take(3) for _ in groups]
    w, sems = take(2)
    me = lax.axis_index("tok")
    a, b, c = me // (2 * inner), (me // 2) % inner, me % 2
    copies, slot = [], 0
    for g, arrays in zip(groups, pieces):
        for (da, db), pair in zip(g["where"], arrays):
            owner = ((a + outer - da) % outer) * inner + (b + inner - db) % inner
            start = pl.multiple_of(owner * 2 * rows, LANES)
            these = []
            for s in range(2):
                for dc, array in enumerate(pair):
                    spot = pl.multiple_of(slot * 2 * rows + ((c + dc) % 2) * rows, LANES)
                    these.append((array.at[s], w.at[s, pl.ds(spot, rows), :]))
            these = [pltpu.make_async_copy(*ends, sems.at[4 * slot + i]) for i, ends in enumerate(these)]
            for copy in these:
                copy.start()
            copies.append((these, pl.ds(start, 2 * rows)))
            slot += 1
    tiles = w.shape[2] // TILE
    slot = 0
    for n, (g, start, total) in enumerate(zip(groups, starts, totals)):
        for first in range(len(g["where"])):
            span = slice(slot * 2 * rows, (slot + 1) * 2 * rows)
            came = start if first == 0 else total
            for s in range(2):
                for copy in copies[slot][0][2 * s : 2 * s + 2]:
                    copy.wait()
                x = x_refs[n][s][:, copies[slot][1]]
                part = jnp.dot(x, w[s, span, :], preferred_element_type=jnp.float32)
                if came is not None:
                    part = came[s][...] + part
                if last and s == 1:
                    part = total[0][...] * part
                    product[...] = part if g is groups[0] else product[...] + part
                else:
                    total[s][...] = part
            for s in range(2):
                for t in range(tiles):
                    one = w[s, span, t * TILE : (t + 1) * TILE]
                    part = lax.dot_general(one, one, (((0,), (0,)), ((), ())), preferred_element_type=jnp.float32)
                    i = s * tiles + t
                    total[2][i] = part if came is None else came[2][i] + part
            slot += 1
    if last:
        columns = w.shape[2]
        row = lax.broadcasted_iota(jnp.int32, (TILE, TILE), 0)
        col = lax.broadcasted_iota(jnp.int32, (TILE, TILE), 1)
        same = row // RANK == col // RANK
        norm = []
        for t in range(tiles):
            both = sum(total[2][t] * total[2][tiles + t] for total in totals)
            norm.append(jnp.sum(jnp.where(same, both, 0.0), axis=0, keepdims=True))
        norm = jnp.broadcast_to(jnp.concatenate(norm, axis=1), (8, columns))
        chooser = group_sums(columns)
        scale = 1.0 / jnp.sqrt(split_dot(norm, chooser)[:1] + 1e-06)
        tokens = product.shape[0]
        cut = tokens // (2 * LANES) * LANES
        outs_now = []
        for i, (low, high) in enumerate(((0, cut), (cut, tokens))):
            scaled = split_dot(product[low:high], chooser) * scale
            token = low + lax.broadcasted_iota(jnp.int32, scaled.shape, 0)
            scaled = jnp.where(token < live_ref[:1], scaled, 0.0)
            made[:, low:high] = scaled.T[: columns // RANK]
            span = pl.ds(low, high - low)
            out = pltpu.make_async_copy(made.at[:, span], outs[0].at[:, span], sems.at[4 * slot + i])
            out.start()
            outs_now.append(out)
        for out in outs_now:
            out.wait()


def stage(shape, groups, live=None):
    last = live is not None
    rows, columns = groups[0]["arrays"][0][0].shape[1:]
    tokens = groups[0]["tokens"][0].shape[0]
    slots = sum(len(g["where"]) for g in groups)
    tiles = 2 * (columns // TILE)
    anywhere = pl.BlockSpec(memory_space=pltpu.HBM)
    vmem = pl.BlockSpec(memory_space=pltpu.VMEM)
    args, specs = [], []
    for g in groups:
        args += g["tokens"]
        specs += [vmem] * 2
    if last:
        args.append(live)
        specs.append(vmem)
    for g in groups:
        for pair in g["arrays"]:
            args += pair
            specs += [anywhere] * 2
    aliases = {}
    for n, g in enumerate(groups):
        if g["carry"] is not None:
            if not last:
                aliases.update({len(args) + i: 3 * n + i for i in range(3)})
            args += list(g["carry"])
            specs += [vmem] * 3
    sums = [((tokens, columns), jnp.float32)] * 2 + [((tiles, TILE, TILE), jnp.float32)]
    scratch = []
    if last:
        out_shape = jax.ShapeDtypeStruct((columns // RANK, tokens), jnp.float32)
        out_specs = anywhere
        scratch = [pltpu.VMEM(*sums[0]), pltpu.VMEM((columns // RANK, tokens), jnp.float32)] + [pltpu.VMEM(*one) for one in sums] * len(groups)
    else:
        out_shape = tuple(jax.ShapeDtypeStruct(*one) for one in sums) * len(groups)
        out_specs = (vmem,) * len(out_shape)
    cfg = dict(
        shape=shape,
        rows=rows,
        last=last,
        groups=[dict(layer=g["layer"], where=g["where"], carry=g["carry"] is not None) for g in groups],
    )
    flops = 4 * slots * rows * columns * (2 * tokens + tiles * TILE)
    return pl.pallas_call(
        functools.partial(stage_kernel, cfg),
        out_shape=out_shape,
        in_specs=specs,
        out_specs=out_specs,
        scratch_shapes=scratch
        + [
            pltpu.VMEM((2, slots * 2 * rows, columns), jnp.bfloat16),
            pltpu.SemaphoreType.DMA((4 * slots + 2,)),
        ],
        input_output_aliases=aliases,
        compiler_params=pltpu.CompilerParams(vmem_limit_bytes=(24 if last else 16) << 20),
        cost_estimate=pl.CostEstimate(
            flops=flops, bytes_accessed=8 * slots * rows * (tokens + columns), transcendentals=0
        ),
    )(*args)


def after(value, *others):
    return lax.optimization_barrier((value,) + others)[0]


def per_device(shape, activations, gradients, query_u, query_v, block_ids, counts):
    outer, inner = shape

    def number(a, b, c):
        return ((a % outer) * inner + b % inner) * 2 + c % 2

    def move(value, da, db, dc):
        steps = [
            (number(a, b, c), number(a + da, b + db, c + dc))
            for a in range(outer)
            for b in range(inner)
            for c in range(2)
        ]
        return lax.ppermute(value, "tok", steps)

    have, pairs = [{}, {}], [{}, {}]
    for layer in range(2):
        have[layer][(0, 0)] = pick(layer, query_u, query_v, block_ids)
    for da in range(outer):
        for layer in range(2):
            h = have[layer]
            if da < outer - 1:
                fed = h[(da, 0)]
                if da:
                    fed = after(fed, h[(da - 1, 1)])
                h[(da + 1, 0)] = move(fed, 1, 0, 0)
            if da == outer - 1 and layer == 1:
                fed = after(h[(0, 1)], have[0][(da, 0)])
                h[(da, 1)] = move(fed, -1, 0, 0)
            else:
                h[(da, 1)] = move(h[(da, 0)], 0, 1, 0)
    for layer in range(2):
        for key, piece in have[layer].items():
            pairs[layer][key] = [piece, move(piece, 0, 0, 1)]

    live, *first = load(0, counts, gradients, activations)
    tokens = [first, load(1, counts, gradients, activations)]

    def group(layer, keys, carry):
        return dict(layer=layer, where=keys, arrays=[pairs[layer][key] for key in keys], carry=carry, tokens=tokens[layer])

    parts = [[(0, 0), (0, 1), (1, 0)]] + [[(da, 1), (da + 1, 0)] for da in range(1, outer - 1)]
    carry = [None, None]
    for keys in parts:
        for layer in range(2):
            carry[layer] = stage(
                shape, [group(layer, keys, carry[layer])])
    scores = stage(shape, [group(layer, [(outer - 1, 1)], carry[layer]) for layer in range(2)], live=live)
    return scores.T


def solution(mesh):
    spec = (
        P(None, ("groups", "tok"), None),
        P(None, ("groups", "tok"), None),
        P("groups", "tok", None),
        P("groups", "tok", None),
        P("groups", None),
        P(("groups", "tok")),
    )
    members = mesh.shape["tok"]
    shape = (OUTER, members // (2 * OUTER))
    ring = members == 4 * OUTER

    def body(*args):
        fits = ring and args[2].shape[1] % LANES == 0
        return per_device(shape, *args) if fits else per_device_plain(*args)

    return jax.shard_map(body, mesh=mesh, in_specs=spec, out_specs=P(("groups", "tok"), None), check_vma=False)
```

```python
import functools

import jax
import jax.numpy as jnp
from jax import lax
from jax.experimental import pallas as pl
from jax.experimental.pallas import tpu as pltpu
from jax.sharding import PartitionSpec as P


RANK = 8
QB = 4
OUTER = 4
LANES = 128
TILE = 256
LOAD_GRANTS = (46 << 20, 45 << 20)


def pick_columns(factor, block_ids):
    width = QB * RANK
    chosen = []
    for layer in range(factor.shape[0]):
        slots = factor[layer].reshape(factor.shape[1], -1, width)
        chosen.append(jnp.take(slots, block_ids[layer], axis=1).reshape(factor.shape[1], -1))
    return jnp.stack(chosen)


def rank_grams(factor):
    per = factor.reshape(factor.shape[0], factor.shape[1], -1, RANK)
    return jnp.einsum("lkqr,lkqs->lqrs", per, per, preferred_element_type=jnp.float32)


def per_device_plain(activations, gradients, query_u, query_v, block_ids, counts):
    layers, tok_rows, _ = activations.shape
    columns = block_ids.shape[1] * QB * RANK
    queries = columns // RANK
    whole_u = lax.all_gather(pick_columns(query_u, block_ids), "tok", axis=1, tiled=True)
    whole_v = lax.all_gather(pick_columns(query_v, block_ids), "tok", axis=1, tiled=True)
    grad_proj = jnp.einsum("ltk,lkc->ltc", gradients, whole_u, preferred_element_type=jnp.float32)
    act_proj = jnp.einsum("ltk,lkc->ltc", activations, whole_v, preferred_element_type=jnp.float32)
    raw = jnp.sum((grad_proj * act_proj).reshape(layers, tok_rows, queries, RANK), axis=(0, 3))
    norm_sq = jnp.sum(rank_grams(whole_u) * rank_grams(whole_v), axis=(0, 2, 3))
    live = jnp.arange(tok_rows, dtype=jnp.int32) < counts[0]
    scaled = raw / jnp.sqrt(norm_sq + 1e-06)[None, :]
    return jnp.where(live[:, None], scaled, jnp.zeros_like(scaled))


def pick_kernel(layer, ids_hbm, u_ref, v_ref, out_ref, ids_ref, held, made, sems):
    width = QB * RANK
    rows = u_ref.shape[1]
    columns = out_ref.shape[2]
    per = LANES // width
    named = pltpu.make_async_copy(ids_hbm, ids_ref, sems.at[4])
    named.start()
    copies = [
        pltpu.make_async_copy(ref.at[layer], held.at[s], sems.at[s]) for s, ref in enumerate((u_ref, v_ref))
    ]
    for copy in copies:
        copy.start()
    named.wait()
    lane = lax.broadcasted_iota(jnp.int32, (rows, LANES), 1) // width
    outs = []
    for s in range(2):
        copies[s].wait()
        for chunk in range(columns // LANES):
            total = None
            for k in range(per):
                stored = ids_ref[layer, chunk * per + k]
                start = pl.multiple_of((stored // per) * LANES, LANES)
                part = held[s, :, pl.ds(start, LANES)].astype(jnp.float32)
                part = pltpu.roll(part, lax.rem(k - stored % per + per, per) * width, 1)
                total = part if total is None else jnp.where(lane == k, part, total)
            made[s, :, chunk * LANES : (chunk + 1) * LANES] = total.astype(jnp.bfloat16)
        out = pltpu.make_async_copy(made.at[s], out_ref.at[s], sems.at[2 + s])
        out.start()
        outs.append(out)
    for out in outs:
        out.wait()


def pick(layer, query_u, query_v, block_ids):
    _, rows, bank = query_u.shape
    columns = block_ids.shape[1] * QB * RANK
    anywhere = pl.BlockSpec(memory_space=pltpu.HBM)
    return pl.pallas_call(
        functools.partial(pick_kernel, layer),
        out_shape=jax.ShapeDtypeStruct((2, rows, columns), jnp.bfloat16),
        in_specs=[anywhere] * 3,
        out_specs=anywhere,
        scratch_shapes=[
            pltpu.SMEM(block_ids.shape, jnp.int32),
            pltpu.VMEM((2, rows, bank), jnp.bfloat16),
            pltpu.VMEM((2, rows, columns), jnp.bfloat16),
            pltpu.SemaphoreType.DMA((5,)),
        ],
        cost_estimate=pl.CostEstimate(
            flops=4 * rows * columns, bytes_accessed=4 * rows * (bank + columns), transcendentals=0
        ),
    )(block_ids, query_u, query_v)


def load_kernel(layer, *refs):
    half = (len(refs) - 2) // 2 if layer == 0 else (len(refs) - 1) // 2
    refs, sems = list(refs[:-1]), refs[-1]
    if layer == 0:
        counts_ref, live_ref = refs.pop(0), refs.pop(half)
    copies = [pltpu.make_async_copy(refs[i].at[layer], refs[half + i], sems.at[i]) for i in range(half)]
    for copy in copies:
        copy.start()
    if layer == 0:
        live_ref[...] = jnp.full(live_ref.shape, counts_ref[0], jnp.int32)
    for copy in copies:
        copy.wait()


def load(layer, counts, *arrays):
    outs = [jax.ShapeDtypeStruct((8, LANES), jnp.int32)] if layer == 0 else []
    outs += [jax.ShapeDtypeStruct(one.shape[1:], one.dtype) for one in arrays]
    specs = [pl.BlockSpec(memory_space=pltpu.SMEM)] if layer == 0 else []
    args = ([counts] if layer == 0 else []) + list(arrays)
    return pl.pallas_call(
        functools.partial(load_kernel, layer),
        out_shape=tuple(outs),
        in_specs=specs + [pl.BlockSpec(memory_space=pltpu.HBM)] * len(arrays),
        out_specs=(pl.BlockSpec(memory_space=pltpu.VMEM),) * len(outs),
        scratch_shapes=[pltpu.SemaphoreType.DMA((len(arrays),))],
        compiler_params=pltpu.CompilerParams(vmem_limit_bytes=LOAD_GRANTS[layer]),
    )(*args)


def split_dot(left, right):
    total = None
    rest = left
    for _ in range(3):
        term = rest.astype(jnp.bfloat16)
        rest = rest - term.astype(jnp.float32)
        part = jnp.dot(term, right, preferred_element_type=jnp.float32)
        total = part if total is None else total + part
    return total


def group_sums(columns):
    row = lax.broadcasted_iota(jnp.int32, (columns, LANES), 0)
    col = lax.broadcasted_iota(jnp.int32, (columns, LANES), 1)
    return jnp.where(row // RANK == col, 1.0, 0.0).astype(jnp.bfloat16)


def stage_kernel(cfg, *refs):
    (outer, inner), groups, last, rows = cfg["shape"], cfg["groups"], cfg["last"], cfg["rows"]
    refs = list(refs)

    def take(n):
        return [refs.pop(0) for _ in range(n)]

    x_refs = [take(2) for _ in groups]
    live_ref = take(1)[0] if last else None
    pieces = [[take(2) for _ in g["where"]] for g in groups]
    starts = [take(3) if g["carry"] else None for g in groups]
    outs = take(1) if last else None
    product = take(1)[0] if last else None
    totals = [take(3) for _ in groups]
    w = take(1)[0]
    me = lax.axis_index("tok")
    a, b, c = me // (2 * inner), (me // 2) % inner, me % 2
    spans, slot = [], 0
    for g, arrays in zip(groups, pieces):
        for (da, db), pair in zip(g["where"], arrays):
            owner = ((a + outer - da) % outer) * inner + (b + inner - db) % inner
            start = pl.multiple_of(owner * 2 * rows, LANES)
            for dc, array in enumerate(pair):
                spot = pl.multiple_of(slot * 2 * rows + ((c + dc) % 2) * rows, LANES)
                w[:, pl.ds(spot, rows), :] = array[...]
            spans.append(pl.ds(start, 2 * rows))
            slot += 1
    tiles = w.shape[2] // TILE
    slot = 0
    for n, (g, start, total) in enumerate(zip(groups, starts, totals)):
        for first in range(len(g["where"])):
            span = slice(slot * 2 * rows, (slot + 1) * 2 * rows)
            came = start if first == 0 else total
            for s in range(2):
                x = x_refs[n][s][:, spans[slot]]
                part = jnp.dot(x, w[s, span, :], preferred_element_type=jnp.float32)
                if came is not None:
                    part = came[s][...] + part
                if last and s == 1:
                    part = total[0][...] * part
                    product[...] = part if g is groups[0] else product[...] + part
                else:
                    total[s][...] = part
            for s in range(2):
                for t in range(tiles):
                    one = w[s, span, t * TILE : (t + 1) * TILE]
                    part = lax.dot_general(one, one, (((0,), (0,)), ((), ())), preferred_element_type=jnp.float32)
                    i = s * tiles + t
                    total[2][i] = part if came is None else came[2][i] + part
            slot += 1
    if last:
        columns = w.shape[2]
        row = lax.broadcasted_iota(jnp.int32, (TILE, TILE), 0)
        col = lax.broadcasted_iota(jnp.int32, (TILE, TILE), 1)
        same = row // RANK == col // RANK
        norm = []
        for t in range(tiles):
            both = sum(total[2][t] * total[2][tiles + t] for total in totals)
            norm.append(jnp.sum(jnp.where(same, both, 0.0), axis=0, keepdims=True))
        norm = jnp.broadcast_to(jnp.concatenate(norm, axis=1), (8, columns))
        chooser = group_sums(columns)
        scale = 1.0 / jnp.sqrt(split_dot(norm, chooser)[:1] + 1e-06)
        scaled = split_dot(product[...], chooser) * scale
        token = lax.broadcasted_iota(jnp.int32, scaled.shape, 0)
        scaled = jnp.where(token < live_ref[:1], scaled, 0.0)
        outs[0][...] = scaled.T[: columns // RANK]


def stage(shape, groups, live=None):
    last = live is not None
    rows, columns = groups[0]["arrays"][0][0].shape[1:]
    tokens = groups[0]["tokens"][0].shape[0]
    slots = sum(len(g["where"]) for g in groups)
    tiles = 2 * (columns // TILE)
    vmem = pl.BlockSpec(memory_space=pltpu.VMEM)
    args, specs = [], []
    for g in groups:
        args += g["tokens"]
        specs += [vmem] * 2
    if last:
        args.append(live)
        specs.append(vmem)
    for g in groups:
        for pair in g["arrays"]:
            args += pair
            specs += [vmem] * 2
    aliases = {}
    for n, g in enumerate(groups):
        if g["carry"] is not None:
            if not last:
                aliases.update({len(args) + i: 3 * n + i for i in range(3)})
            args += list(g["carry"])
            specs += [vmem] * 3
    sums = [((tokens, columns), jnp.float32)] * 2 + [((tiles, TILE, TILE), jnp.float32)]
    scratch = []
    if last:
        out_shape = jax.ShapeDtypeStruct((columns // RANK, tokens), jnp.float32)
        out_specs = vmem
        scratch = [pltpu.VMEM(*sums[0])] + [pltpu.VMEM(*one) for one in sums] * len(groups)
    else:
        out_shape = tuple(jax.ShapeDtypeStruct(*one) for one in sums) * len(groups)
        out_specs = (vmem,) * len(out_shape)
    cfg = dict(
        shape=shape,
        rows=rows,
        last=last,
        groups=[dict(layer=g["layer"], where=g["where"], carry=g["carry"] is not None) for g in groups],
    )
    flops = 4 * slots * rows * columns * (2 * tokens + tiles * TILE)
    return pl.pallas_call(
        functools.partial(stage_kernel, cfg),
        out_shape=out_shape,
        in_specs=specs,
        out_specs=out_specs,
        scratch_shapes=scratch + [pltpu.VMEM((2, slots * 2 * rows, columns), jnp.bfloat16)],
        input_output_aliases=aliases,
        compiler_params=pltpu.CompilerParams(vmem_limit_bytes=(24 if last else 16) << 20),
        cost_estimate=pl.CostEstimate(
            flops=flops, bytes_accessed=8 * slots * rows * (tokens + columns), transcendentals=0
        ),
    )(*args)


def after(value, *others):
    return lax.optimization_barrier((value,) + others)[0]


def per_device(shape, activations, gradients, query_u, query_v, block_ids, counts):
    outer, inner = shape

    def number(a, b, c):
        return ((a % outer) * inner + b % inner) * 2 + c % 2

    def move(value, da, db, dc):
        steps = [
            (number(a, b, c), number(a + da, b + db, c + dc))
            for a in range(outer)
            for b in range(inner)
            for c in range(2)
        ]
        return lax.ppermute(value, "tok", steps)

    have, pairs = [{}, {}], [{}, {}]
    for layer in range(2):
        have[layer][(0, 0)] = pick(layer, query_u, query_v, block_ids)
    for da in range(outer):
        for layer in range(2):
            h = have[layer]
            if da < outer - 1:
                fed = h[(da, 0)]
                if da:
                    fed = after(fed, h[(da - 1, 1)])
                h[(da + 1, 0)] = move(fed, 1, 0, 0)
            if da == outer - 1 and layer == 1:
                fed = after(h[(0, 1)], have[0][(da, 0)])
                h[(da, 1)] = move(fed, -1, 0, 0)
            else:
                h[(da, 1)] = move(h[(da, 0)], 0, 1, 0)
    for layer in range(2):
        for key, piece in have[layer].items():
            pairs[layer][key] = [piece, move(piece, 0, 0, 1)]

    live, *first = load(0, counts, gradients, activations)
    tokens = [first, load(1, counts, gradients, activations)]

    def group(layer, keys, carry):
        return dict(layer=layer, where=keys, arrays=[pairs[layer][key] for key in keys], carry=carry, tokens=tokens[layer])

    parts = [[(0, 0), (0, 1), (1, 0)]] + [[(da, 1), (da + 1, 0)] for da in range(1, outer - 1)]
    carry = [None, None]
    for keys in parts:
        for layer in range(2):
            carry[layer] = stage(
                shape, [group(layer, keys, carry[layer])])
    scores = stage(shape, [group(layer, [(outer - 1, 1)], carry[layer]) for layer in range(2)], live=live)
    return scores.T


def solution(mesh):
    spec = (
        P(None, ("groups", "tok"), None),
        P(None, ("groups", "tok"), None),
        P("groups", "tok", None),
        P("groups", "tok", None),
        P("groups", None),
        P(("groups", "tok")),
    )
    members = mesh.shape["tok"]
    shape = (OUTER, members // (2 * OUTER))
    ring = members == 4 * OUTER

    def body(*args):
        fits = ring and args[2].shape[1] % LANES == 0
        return per_device(shape, *args) if fits else per_device_plain(*args)

    return jax.shard_map(body, mesh=mesh, in_specs=spec, out_specs=P(("groups", "tok"), None), check_vma=False)
```

```python
import functools

import jax
import jax.numpy as jnp
from jax import lax
from jax.experimental import pallas as pl
from jax.experimental.pallas import tpu as pltpu
from jax.sharding import PartitionSpec as P


RANK = 8
QB = 4
OUTER = 4
LANES = 128
TILE = 256
TERMS = 2
LOAD_GRANTS = (46 << 20, 45 << 20)


def pick_columns(factor, block_ids):
    width = QB * RANK
    chosen = []
    for layer in range(factor.shape[0]):
        slots = factor[layer].reshape(factor.shape[1], -1, width)
        chosen.append(jnp.take(slots, block_ids[layer], axis=1).reshape(factor.shape[1], -1))
    return jnp.stack(chosen)


def rank_grams(factor):
    per = factor.reshape(factor.shape[0], factor.shape[1], -1, RANK)
    return jnp.einsum("lkqr,lkqs->lqrs", per, per, preferred_element_type=jnp.float32)


def per_device_plain(activations, gradients, query_u, query_v, block_ids, counts):
    layers, tok_rows, _ = activations.shape
    columns = block_ids.shape[1] * QB * RANK
    queries = columns // RANK
    whole_u = lax.all_gather(pick_columns(query_u, block_ids), "tok", axis=1, tiled=True)
    whole_v = lax.all_gather(pick_columns(query_v, block_ids), "tok", axis=1, tiled=True)
    grad_proj = jnp.einsum("ltk,lkc->ltc", gradients, whole_u, preferred_element_type=jnp.float32)
    act_proj = jnp.einsum("ltk,lkc->ltc", activations, whole_v, preferred_element_type=jnp.float32)
    raw = jnp.sum((grad_proj * act_proj).reshape(layers, tok_rows, queries, RANK), axis=(0, 3))
    norm_sq = jnp.sum(rank_grams(whole_u) * rank_grams(whole_v), axis=(0, 2, 3))
    live = jnp.arange(tok_rows, dtype=jnp.int32) < counts[0]
    scaled = raw / jnp.sqrt(norm_sq + 1e-06)[None, :]
    return jnp.where(live[:, None], scaled, jnp.zeros_like(scaled))


def pick_kernel(layer, ids_hbm, u_ref, v_ref, out_ref, ids_ref, held, made, sems):
    width = QB * RANK
    rows = u_ref.shape[1]
    columns = out_ref.shape[2]
    per = LANES // width
    named = pltpu.make_async_copy(ids_hbm, ids_ref, sems.at[4])
    named.start()
    copies = [
        pltpu.make_async_copy(ref.at[layer], held.at[s], sems.at[s]) for s, ref in enumerate((u_ref, v_ref))
    ]
    for copy in copies:
        copy.start()
    named.wait()
    lane = lax.broadcasted_iota(jnp.int32, (rows, LANES), 1) // width
    outs = []
    for s in range(2):
        copies[s].wait()
        for chunk in range(columns // LANES):
            total = None
            for k in range(per):
                stored = ids_ref[layer, chunk * per + k]
                start = pl.multiple_of((stored // per) * LANES, LANES)
                part = held[s, :, pl.ds(start, LANES)].astype(jnp.float32)
                part = pltpu.roll(part, lax.rem(k - stored % per + per, per) * width, 1)
                total = part if total is None else jnp.where(lane == k, part, total)
            made[s, :, chunk * LANES : (chunk + 1) * LANES] = total.astype(jnp.bfloat16)
        out = pltpu.make_async_copy(made.at[s], out_ref.at[s], sems.at[2 + s])
        out.start()
        outs.append(out)
    for out in outs:
        out.wait()


def pick(layer, query_u, query_v, block_ids):
    _, rows, bank = query_u.shape
    columns = block_ids.shape[1] * QB * RANK
    anywhere = pl.BlockSpec(memory_space=pltpu.HBM)
    return pl.pallas_call(
        functools.partial(pick_kernel, layer),
        out_shape=jax.ShapeDtypeStruct((2, rows, columns), jnp.bfloat16),
        in_specs=[anywhere] * 3,
        out_specs=anywhere,
        scratch_shapes=[
            pltpu.SMEM(block_ids.shape, jnp.int32),
            pltpu.VMEM((2, rows, bank), jnp.bfloat16),
            pltpu.VMEM((2, rows, columns), jnp.bfloat16),
            pltpu.SemaphoreType.DMA((5,)),
        ],
        cost_estimate=pl.CostEstimate(
            flops=4 * rows * columns, bytes_accessed=4 * rows * (bank + columns), transcendentals=0
        ),
    )(block_ids, query_u, query_v)


def load_kernel(layer, *refs):
    half = (len(refs) - 2) // 2 if layer == 0 else (len(refs) - 1) // 2
    refs, sems = list(refs[:-1]), refs[-1]
    if layer == 0:
        counts_ref, live_ref = refs.pop(0), refs.pop(half)
    copies = [pltpu.make_async_copy(refs[i].at[layer], refs[half + i], sems.at[i]) for i in range(half)]
    for copy in copies:
        copy.start()
    if layer == 0:
        live_ref[...] = jnp.full(live_ref.shape, counts_ref[0], jnp.int32)
    for copy in copies:
        copy.wait()


def load(layer, counts, *arrays):
    outs = [jax.ShapeDtypeStruct((8, LANES), jnp.int32)] if layer == 0 else []
    outs += [jax.ShapeDtypeStruct(one.shape[1:], one.dtype) for one in arrays]
    specs = [pl.BlockSpec(memory_space=pltpu.SMEM)] if layer == 0 else []
    args = ([counts] if layer == 0 else []) + list(arrays)
    return pl.pallas_call(
        functools.partial(load_kernel, layer),
        out_shape=tuple(outs),
        in_specs=specs + [pl.BlockSpec(memory_space=pltpu.HBM)] * len(arrays),
        out_specs=(pl.BlockSpec(memory_space=pltpu.VMEM),) * len(outs),
        scratch_shapes=[pltpu.SemaphoreType.DMA((len(arrays),))],
        compiler_params=pltpu.CompilerParams(vmem_limit_bytes=LOAD_GRANTS[layer]),
    )(*args)


def split_dot(left, right):
    total = None
    rest = left
    for _ in range(TERMS):
        term = rest.astype(jnp.bfloat16)
        rest = rest - term.astype(jnp.float32)
        part = jnp.dot(term, right, preferred_element_type=jnp.float32)
        total = part if total is None else total + part
    return total


def group_sums(columns):
    row = lax.broadcasted_iota(jnp.int32, (columns, LANES), 0)
    col = lax.broadcasted_iota(jnp.int32, (columns, LANES), 1)
    return jnp.where(row // RANK == col, 1.0, 0.0).astype(jnp.bfloat16)


def stage_kernel(cfg, *refs):
    (outer, inner), groups, last, rows = cfg["shape"], cfg["groups"], cfg["last"], cfg["rows"]
    refs = list(refs)

    def take(n):
        return [refs.pop(0) for _ in range(n)]

    x_refs = [take(2) for _ in groups]
    live_ref = take(1)[0] if last else None
    pieces = [[take(2) for _ in g["where"]] for g in groups]
    starts = [take(3) if g["carry"] else None for g in groups]
    outs = take(1) if last else None
    product = take(1)[0] if last else None
    totals = [take(3) for _ in groups]
    w = take(1)[0]
    me = lax.axis_index("tok")
    a, b, c = me // (2 * inner), (me // 2) % inner, me % 2
    spans, slot = [], 0
    for g, arrays in zip(groups, pieces):
        for (da, db), pair in zip(g["where"], arrays):
            owner = ((a + outer - da) % outer) * inner + (b + inner - db) % inner
            start = pl.multiple_of(owner * 2 * rows, LANES)
            for dc, array in enumerate(pair):
                spot = pl.multiple_of(slot * 2 * rows + ((c + dc) % 2) * rows, LANES)
                w[:, pl.ds(spot, rows), :] = array[...]
            spans.append(pl.ds(start, 2 * rows))
            slot += 1
    tiles = w.shape[2] // TILE
    slot = 0
    for n, (g, start, total) in enumerate(zip(groups, starts, totals)):
        for first in range(len(g["where"])):
            span = slice(slot * 2 * rows, (slot + 1) * 2 * rows)
            came = start if first == 0 else total
            for s in range(2):
                x = x_refs[n][s][:, spans[slot]]
                part = jnp.dot(x, w[s, span, :], preferred_element_type=jnp.float32)
                if came is not None:
                    part = came[s][...] + part
                if last and s == 1:
                    part = total[0][...] * part
                    product[...] = part if g is groups[0] else product[...] + part
                else:
                    total[s][...] = part
            for s in range(2):
                for t in range(tiles):
                    one = w[s, span, t * TILE : (t + 1) * TILE]
                    part = lax.dot_general(one, one, (((0,), (0,)), ((), ())), preferred_element_type=jnp.float32)
                    i = s * tiles + t
                    total[2][i] = part if came is None else came[2][i] + part
            slot += 1
    if last:
        columns = w.shape[2]
        row = lax.broadcasted_iota(jnp.int32, (TILE, TILE), 0)
        col = lax.broadcasted_iota(jnp.int32, (TILE, TILE), 1)
        same = row // RANK == col // RANK
        norm = []
        for t in range(tiles):
            both = sum(total[2][t] * total[2][tiles + t] for total in totals)
            norm.append(jnp.sum(jnp.where(same, both, 0.0), axis=0, keepdims=True))
        norm = jnp.broadcast_to(jnp.concatenate(norm, axis=1), (8, columns))
        chooser = group_sums(columns)
        scale = 1.0 / jnp.sqrt(split_dot(norm, chooser)[:1] + 1e-06)
        tokens = product.shape[0]
        for low in range(0, tokens, LANES):
            span = slice(low, low + LANES)
            rest, terms = product[span], []
            for _ in range(TERMS):
                terms.append(rest.astype(jnp.bfloat16))
                rest = rest - terms[-1].astype(jnp.float32)
            raw = jnp.dot(jnp.concatenate(terms, axis=0), chooser, preferred_element_type=jnp.float32)
            raw = sum(raw[i * LANES : (i + 1) * LANES] for i in range(TERMS))
            token = low + lax.broadcasted_iota(jnp.int32, raw.shape, 0)
            scaled = jnp.where(token < live_ref[:1], raw * scale, 0.0)
            outs[0][:, span] = scaled.T[: columns // RANK]


def stage(shape, groups, live=None):
    last = live is not None
    rows, columns = groups[0]["arrays"][0][0].shape[1:]
    tokens = groups[0]["tokens"][0].shape[0]
    slots = sum(len(g["where"]) for g in groups)
    tiles = 2 * (columns // TILE)
    vmem = pl.BlockSpec(memory_space=pltpu.VMEM)
    args, specs = [], []
    for g in groups:
        args += g["tokens"]
        specs += [vmem] * 2
    if last:
        args.append(live)
        specs.append(vmem)
    for g in groups:
        for pair in g["arrays"]:
            args += pair
            specs += [vmem] * 2
    aliases = {}
    for n, g in enumerate(groups):
        if g["carry"] is not None:
            if not last:
                aliases.update({len(args) + i: 3 * n + i for i in range(3)})
            args += list(g["carry"])
            specs += [vmem] * 3
    sums = [((tokens, columns), jnp.float32)] * 2 + [((tiles, TILE, TILE), jnp.float32)]
    scratch = []
    if last:
        out_shape = jax.ShapeDtypeStruct((columns // RANK, tokens), jnp.float32)
        out_specs = vmem
        scratch = [pltpu.VMEM(*sums[0])] + [pltpu.VMEM(*one) for one in sums] * len(groups)
    else:
        out_shape = tuple(jax.ShapeDtypeStruct(*one) for one in sums) * len(groups)
        out_specs = (vmem,) * len(out_shape)
    cfg = dict(
        shape=shape,
        rows=rows,
        last=last,
        groups=[dict(layer=g["layer"], where=g["where"], carry=g["carry"] is not None) for g in groups],
    )
    flops = 4 * slots * rows * columns * (2 * tokens + tiles * TILE)
    return pl.pallas_call(
        functools.partial(stage_kernel, cfg),
        out_shape=out_shape,
        in_specs=specs,
        out_specs=out_specs,
        scratch_shapes=scratch + [pltpu.VMEM((2, slots * 2 * rows, columns), jnp.bfloat16)],
        input_output_aliases=aliases,
        compiler_params=pltpu.CompilerParams(vmem_limit_bytes=(24 if last else 16) << 20),
        cost_estimate=pl.CostEstimate(
            flops=flops, bytes_accessed=8 * slots * rows * (tokens + columns), transcendentals=0
        ),
    )(*args)


def after(value, *others):
    return lax.optimization_barrier((value,) + others)[0]


def per_device(shape, activations, gradients, query_u, query_v, block_ids, counts):
    outer, inner = shape

    def number(a, b, c):
        return ((a % outer) * inner + b % inner) * 2 + c % 2

    def move(value, da, db, dc):
        steps = [
            (number(a, b, c), number(a + da, b + db, c + dc))
            for a in range(outer)
            for b in range(inner)
            for c in range(2)
        ]
        return lax.ppermute(value, "tok", steps)

    have, pairs = [{}, {}], [{}, {}]
    for layer in range(2):
        have[layer][(0, 0)] = pick(layer, query_u, query_v, block_ids)
    for da in range(outer):
        for layer in range(2):
            h = have[layer]
            if da < outer - 1:
                fed = h[(da, 0)]
                if da:
                    fed = after(fed, h[(da - 1, 1)])
                h[(da + 1, 0)] = move(fed, 1, 0, 0)
            if da == outer - 1 and layer == 1:
                fed = after(h[(0, 1)], have[0][(da, 0)])
                h[(da, 1)] = move(fed, -1, 0, 0)
            else:
                h[(da, 1)] = move(h[(da, 0)], 0, 1, 0)
    for layer in range(2):
        for key, piece in have[layer].items():
            pairs[layer][key] = [piece, move(piece, 0, 0, 1)]

    live, *first = load(0, counts, gradients, activations)
    tokens = [first, load(1, counts, gradients, activations)]

    def group(layer, keys, carry):
        return dict(layer=layer, where=keys, arrays=[pairs[layer][key] for key in keys], carry=carry, tokens=tokens[layer])

    parts = [[(0, 0), (0, 1), (1, 0)]] + [[(da, 1), (da + 1, 0)] for da in range(1, outer - 1)]
    carry = [None, None]
    for keys in parts:
        for layer in range(2):
            carry[layer] = stage(
                shape, [group(layer, keys, carry[layer])])
    scores = stage(shape, [group(layer, [(outer - 1, 1)], carry[layer]) for layer in range(2)], live=live)
    return scores.T


def solution(mesh):
    spec = (
        P(None, ("groups", "tok"), None),
        P(None, ("groups", "tok"), None),
        P("groups", "tok", None),
        P("groups", "tok", None),
        P("groups", None),
        P(("groups", "tok")),
    )
    members = mesh.shape["tok"]
    shape = (OUTER, members // (2 * OUTER))
    ring = members == 4 * OUTER

    def body(*args):
        fits = ring and args[2].shape[1] % LANES == 0
        return per_device(shape, *args) if fits else per_device_plain(*args)

    return jax.shard_map(body, mesh=mesh, in_specs=spec, out_specs=P(("groups", "tok"), None), check_vma=False)
```

```python
import functools

import jax
import jax.numpy as jnp
from jax import lax
from jax.experimental import pallas as pl
from jax.experimental.pallas import tpu as pltpu
from jax.sharding import PartitionSpec as P


RANK = 8
QB = 4
OUTER = 4
LANES = 128
TILE = 256
TERMS = 2
GRANT = 24 << 20


def pick_columns(factor, block_ids):
    width = QB * RANK
    chosen = []
    for layer in range(factor.shape[0]):
        slots = factor[layer].reshape(factor.shape[1], -1, width)
        chosen.append(jnp.take(slots, block_ids[layer], axis=1).reshape(factor.shape[1], -1))
    return jnp.stack(chosen)


def rank_grams(factor):
    per = factor.reshape(factor.shape[0], factor.shape[1], -1, RANK)
    return jnp.einsum("lkqr,lkqs->lqrs", per, per, preferred_element_type=jnp.float32)


def per_device_plain(activations, gradients, query_u, query_v, block_ids, counts):
    layers, tok_rows, _ = activations.shape
    columns = block_ids.shape[1] * QB * RANK
    queries = columns // RANK
    whole_u = lax.all_gather(pick_columns(query_u, block_ids), "tok", axis=1, tiled=True)
    whole_v = lax.all_gather(pick_columns(query_v, block_ids), "tok", axis=1, tiled=True)
    grad_proj = jnp.einsum("ltk,lkc->ltc", gradients, whole_u, preferred_element_type=jnp.float32)
    act_proj = jnp.einsum("ltk,lkc->ltc", activations, whole_v, preferred_element_type=jnp.float32)
    raw = jnp.sum((grad_proj * act_proj).reshape(layers, tok_rows, queries, RANK), axis=(0, 3))
    norm_sq = jnp.sum(rank_grams(whole_u) * rank_grams(whole_v), axis=(0, 2, 3))
    live = jnp.arange(tok_rows, dtype=jnp.int32) < counts[0]
    scaled = raw / jnp.sqrt(norm_sq + 1e-06)[None, :]
    return jnp.where(live[:, None], scaled, jnp.zeros_like(scaled))


def pick_kernel(layer, ids_hbm, u_ref, v_ref, out_ref, ids_ref, held, sems):
    width = QB * RANK
    rows = u_ref.shape[1]
    columns = out_ref.shape[2]
    per = LANES // width
    named = pltpu.make_async_copy(ids_hbm, ids_ref, sems.at[4])
    named.start()
    copies = [
        pltpu.make_async_copy(ref.at[layer], held.at[s], sems.at[s]) for s, ref in enumerate((u_ref, v_ref))
    ]
    for copy in copies:
        copy.start()
    named.wait()
    lane = lax.broadcasted_iota(jnp.int32, (rows, LANES), 1) // width
    for s in range(2):
        copies[s].wait()
        for chunk in range(columns // LANES):
            total = None
            for k in range(per):
                stored = ids_ref[layer, chunk * per + k]
                start = pl.multiple_of((stored // per) * LANES, LANES)
                part = held[s, :, pl.ds(start, LANES)].astype(jnp.float32)
                part = pltpu.roll(part, lax.rem(k - stored % per + per, per) * width, 1)
                total = part if total is None else jnp.where(lane == k, part, total)
            out_ref[s, :, chunk * LANES : (chunk + 1) * LANES] = total.astype(jnp.bfloat16)


def in_hbm(*arrays):
    return [pltpu.with_memory_space_constraint(one, pltpu.HBM) for one in arrays]


def pick(layer, query_u, query_v, block_ids):
    _, rows, bank = query_u.shape
    columns = block_ids.shape[1] * QB * RANK
    anywhere = pl.BlockSpec(memory_space=pltpu.HBM)
    return pl.pallas_call(
        functools.partial(pick_kernel, layer),
        out_shape=jax.ShapeDtypeStruct((2, rows, columns), jnp.bfloat16),
        in_specs=[anywhere] * 3,
        out_specs=pl.BlockSpec(memory_space=pltpu.VMEM),
        scratch_shapes=[
            pltpu.SMEM(block_ids.shape, jnp.int32),
            pltpu.VMEM((2, rows, bank), jnp.bfloat16),
            pltpu.SemaphoreType.DMA((5,)),
        ],
        compiler_params=pltpu.CompilerParams(vmem_limit_bytes=GRANT),
        cost_estimate=pl.CostEstimate(
            flops=4 * rows * columns, bytes_accessed=4 * rows * (bank + columns), transcendentals=0
        ),
    )(*in_hbm(block_ids, query_u, query_v))


def load_kernel(layer, *refs):
    half = (len(refs) - 2) // 2 if layer == 0 else (len(refs) - 1) // 2
    refs, sems = list(refs[:-1]), refs[-1]
    if layer == 0:
        counts_ref, live_ref = refs.pop(0), refs.pop(half)
    copies = [pltpu.make_async_copy(refs[i].at[layer], refs[half + i], sems.at[i]) for i in range(half)]
    for copy in copies:
        copy.start()
    if layer == 0:
        live_ref[...] = jnp.full(live_ref.shape, counts_ref[0], jnp.int32)
    for copy in copies:
        copy.wait()


def load(layer, counts, *arrays):
    outs = [jax.ShapeDtypeStruct((8, LANES), jnp.int32)] if layer == 0 else []
    outs += [jax.ShapeDtypeStruct(one.shape[1:], one.dtype) for one in arrays]
    specs = [pl.BlockSpec(memory_space=pltpu.SMEM)] if layer == 0 else []
    args = ([counts] if layer == 0 else []) + in_hbm(*arrays)
    return pl.pallas_call(
        functools.partial(load_kernel, layer),
        out_shape=tuple(outs),
        in_specs=specs + [pl.BlockSpec(memory_space=pltpu.HBM)] * len(arrays),
        out_specs=(pl.BlockSpec(memory_space=pltpu.VMEM),) * len(outs),
        scratch_shapes=[pltpu.SemaphoreType.DMA((len(arrays),))],
        compiler_params=pltpu.CompilerParams(vmem_limit_bytes=GRANT),
    )(*args)


def split_dot(left, right):
    total = None
    rest = left
    for _ in range(TERMS):
        term = rest.astype(jnp.bfloat16)
        rest = rest - term.astype(jnp.float32)
        part = jnp.dot(term, right, preferred_element_type=jnp.float32)
        total = part if total is None else total + part
    return total


def group_sums(columns):
    row = lax.broadcasted_iota(jnp.int32, (columns, LANES), 0)
    col = lax.broadcasted_iota(jnp.int32, (columns, LANES), 1)
    return jnp.where(row // RANK == col, 1.0, 0.0).astype(jnp.bfloat16)


def stage_kernel(cfg, *refs):
    (outer, inner), groups, last, rows = cfg["shape"], cfg["groups"], cfg["last"], cfg["rows"]
    refs = list(refs)

    def take(n):
        return [refs.pop(0) for _ in range(n)]

    x_refs = [take(2) for _ in groups]
    live_ref = take(1)[0] if last else None
    pieces = [[take(2) for _ in g["where"]] for g in groups]
    starts = [take(3) if g["carry"] else None for g in groups]
    outs = take(1) if last else None
    product = take(1)[0] if last else None
    totals = [take(3) for _ in groups]
    w = take(1)[0]
    me = lax.axis_index("tok")
    a, b, c = me // (2 * inner), (me // 2) % inner, me % 2
    spans, slot = [], 0
    for g, arrays in zip(groups, pieces):
        for (da, db), pair in zip(g["where"], arrays):
            owner = ((a + outer - da) % outer) * inner + (b + inner - db) % inner
            start = pl.multiple_of(owner * 2 * rows, LANES)
            for dc, array in enumerate(pair):
                spot = pl.multiple_of(slot * 2 * rows + ((c + dc) % 2) * rows, LANES)
                w[:, pl.ds(spot, rows), :] = array[...]
            spans.append(pl.ds(start, 2 * rows))
            slot += 1
    tiles = w.shape[2] // TILE
    slot = 0
    for n, (g, start, total) in enumerate(zip(groups, starts, totals)):
        for first in range(len(g["where"])):
            span = slice(slot * 2 * rows, (slot + 1) * 2 * rows)
            came = start if first == 0 else total
            for s in range(2):
                x = x_refs[n][s][:, spans[slot]]
                part = jnp.dot(x, w[s, span, :], preferred_element_type=jnp.float32)
                if came is not None:
                    part = came[s][...] + part
                if last and s == 1:
                    part = total[0][...] * part
                    product[...] = part if g is groups[0] else product[...] + part
                else:
                    total[s][...] = part
            for s in range(2):
                for t in range(tiles):
                    one = w[s, span, t * TILE : (t + 1) * TILE]
                    part = lax.dot_general(one, one, (((0,), (0,)), ((), ())), preferred_element_type=jnp.float32)
                    i = s * tiles + t
                    total[2][i] = part if came is None else came[2][i] + part
            slot += 1
    if last:
        columns = w.shape[2]
        row = lax.broadcasted_iota(jnp.int32, (TILE, TILE), 0)
        col = lax.broadcasted_iota(jnp.int32, (TILE, TILE), 1)
        same = row // RANK == col // RANK
        norm = []
        for t in range(tiles):
            both = sum(total[2][t] * total[2][tiles + t] for total in totals)
            norm.append(jnp.sum(jnp.where(same, both, 0.0), axis=0, keepdims=True))
        norm = jnp.broadcast_to(jnp.concatenate(norm, axis=1), (8, columns))
        chooser = group_sums(columns)
        scale = 1.0 / jnp.sqrt(split_dot(norm, chooser)[:1] + 1e-06)
        tokens = product.shape[0]
        for low in range(0, tokens, LANES):
            span = slice(low, low + LANES)
            rest, terms = product[span], []
            for _ in range(TERMS):
                terms.append(rest.astype(jnp.bfloat16))
                rest = rest - terms[-1].astype(jnp.float32)
            raw = jnp.dot(jnp.concatenate(terms, axis=0), chooser, preferred_element_type=jnp.float32)
            raw = sum(raw[i * LANES : (i + 1) * LANES] for i in range(TERMS))
            token = low + lax.broadcasted_iota(jnp.int32, raw.shape, 0)
            scaled = jnp.where(token < live_ref[:1], raw * scale, 0.0)
            outs[0][:, span] = scaled.T[: columns // RANK]


def stage(shape, groups, live=None):
    last = live is not None
    rows, columns = groups[0]["arrays"][0][0].shape[1:]
    tokens = groups[0]["tokens"][0].shape[0]
    slots = sum(len(g["where"]) for g in groups)
    tiles = 2 * (columns // TILE)
    vmem = pl.BlockSpec(memory_space=pltpu.VMEM)
    args, specs = [], []
    for g in groups:
        args += g["tokens"]
        specs += [vmem] * 2
    if last:
        args.append(live)
        specs.append(vmem)
    for g in groups:
        for pair in g["arrays"]:
            args += pair
            specs += [vmem] * 2
    aliases = {}
    for n, g in enumerate(groups):
        if g["carry"] is not None:
            if not last:
                aliases.update({len(args) + i: 3 * n + i for i in range(3)})
            args += list(g["carry"])
            specs += [vmem] * 3
    sums = [((tokens, columns), jnp.float32)] * 2 + [((tiles, TILE, TILE), jnp.float32)]
    scratch = []
    if last:
        out_shape = jax.ShapeDtypeStruct((columns // RANK, tokens), jnp.float32)
        out_specs = vmem
        scratch = [pltpu.VMEM(*sums[0])] + [pltpu.VMEM(*one) for one in sums] * len(groups)
    else:
        out_shape = tuple(jax.ShapeDtypeStruct(*one) for one in sums) * len(groups)
        out_specs = (vmem,) * len(out_shape)
    cfg = dict(
        shape=shape,
        rows=rows,
        last=last,
        groups=[dict(layer=g["layer"], where=g["where"], carry=g["carry"] is not None) for g in groups],
    )
    flops = 4 * slots * rows * columns * (2 * tokens + tiles * TILE)
    return pl.pallas_call(
        functools.partial(stage_kernel, cfg),
        out_shape=out_shape,
        in_specs=specs,
        out_specs=out_specs,
        scratch_shapes=scratch + [pltpu.VMEM((2, slots * 2 * rows, columns), jnp.bfloat16)],
        input_output_aliases=aliases,
        compiler_params=pltpu.CompilerParams(vmem_limit_bytes=GRANT),
        cost_estimate=pl.CostEstimate(
            flops=flops, bytes_accessed=8 * slots * rows * (tokens + columns), transcendentals=0
        ),
    )(*args)


def after(value, *others):
    return lax.optimization_barrier((value,) + others)[0]


def per_device(shape, activations, gradients, query_u, query_v, block_ids, counts):
    outer, inner = shape

    def number(a, b, c):
        return ((a % outer) * inner + b % inner) * 2 + c % 2

    def move(value, da, db, dc):
        steps = [
            (number(a, b, c), number(a + da, b + db, c + dc))
            for a in range(outer)
            for b in range(inner)
            for c in range(2)
        ]
        return lax.ppermute(value, "tok", steps)

    have, pairs = [{}, {}], [{}, {}]
    for layer in range(2):
        have[layer][(0, 0)] = pick(layer, query_u, query_v, block_ids)
    for da in range(outer):
        for layer in range(2):
            h = have[layer]
            if da < outer - 1:
                fed = h[(da, 0)]
                h[(da + 1, 0)] = move(fed, 1, 0, 0)
            if da == outer - 1 and layer == 1:
                fed = after(h[(0, 1)], have[0][(da, 0)])
                h[(da, 1)] = move(fed, -1, 0, 0)
            else:
                h[(da, 1)] = move(h[(da, 0)], 0, 1, 0)
    for layer in range(2):
        for key, piece in have[layer].items():
            pairs[layer][key] = [piece, move(piece, 0, 0, 1)]

    live, *first = load(0, counts, gradients, activations)
    tokens = [first, load(1, counts, gradients, activations)]

    def group(layer, keys, carry):
        return dict(layer=layer, where=keys, arrays=[pairs[layer][key] for key in keys], carry=carry, tokens=tokens[layer])

    parts = [[(0, 0), (0, 1), (1, 0)]] + [[(da, 1), (da + 1, 0)] for da in range(1, outer - 1)]
    carry = [None, None]
    for keys in parts:
        for layer in range(2):
            carry[layer] = stage(
                shape, [group(layer, keys, carry[layer])])
    scores = stage(shape, [group(layer, [(outer - 1, 1)], carry[layer]) for layer in range(2)], live=live)
    return scores.T


def solution(mesh):
    spec = (
        P(None, ("groups", "tok"), None),
        P(None, ("groups", "tok"), None),
        P("groups", "tok", None),
        P("groups", "tok", None),
        P("groups", None),
        P(("groups", "tok")),
    )
    members = mesh.shape["tok"]
    shape = (OUTER, members // (2 * OUTER))
    ring = members == 4 * OUTER

    def body(*args):
        fits = ring and args[2].shape[1] % LANES == 0
        return per_device(shape, *args) if fits else per_device_plain(*args)

    return jax.shard_map(body, mesh=mesh, in_specs=spec, out_specs=P(("groups", "tok"), None), check_vma=False)
```

```python
import functools

import jax
import jax.numpy as jnp
from jax import lax
from jax.experimental import pallas as pl
from jax.experimental.pallas import tpu as pltpu
from jax.sharding import PartitionSpec as P


RANK = 8
QB = 4
OUTER = 4
LANES = 128
TILE = 256
TERMS = 2
GRANT = 24 << 20


def pick_columns(factor, block_ids):
    width = QB * RANK
    chosen = []
    for layer in range(factor.shape[0]):
        slots = factor[layer].reshape(factor.shape[1], -1, width)
        chosen.append(jnp.take(slots, block_ids[layer], axis=1).reshape(factor.shape[1], -1))
    return jnp.stack(chosen)


def rank_grams(factor):
    per = factor.reshape(factor.shape[0], factor.shape[1], -1, RANK)
    return jnp.einsum("lkqr,lkqs->lqrs", per, per, preferred_element_type=jnp.float32)


def per_device_plain(activations, gradients, query_u, query_v, block_ids, counts):
    layers, tok_rows, _ = activations.shape
    columns = block_ids.shape[1] * QB * RANK
    queries = columns // RANK
    whole_u = lax.all_gather(pick_columns(query_u, block_ids), "tok", axis=1, tiled=True)
    whole_v = lax.all_gather(pick_columns(query_v, block_ids), "tok", axis=1, tiled=True)
    grad_proj = jnp.einsum("ltk,lkc->ltc", gradients, whole_u, preferred_element_type=jnp.float32)
    act_proj = jnp.einsum("ltk,lkc->ltc", activations, whole_v, preferred_element_type=jnp.float32)
    raw = jnp.sum((grad_proj * act_proj).reshape(layers, tok_rows, queries, RANK), axis=(0, 3))
    norm_sq = jnp.sum(rank_grams(whole_u) * rank_grams(whole_v), axis=(0, 2, 3))
    live = jnp.arange(tok_rows, dtype=jnp.int32) < counts[0]
    scaled = raw / jnp.sqrt(norm_sq + 1e-06)[None, :]
    return jnp.where(live[:, None], scaled, jnp.zeros_like(scaled))


def pick_kernel(layer, ids_hbm, u_ref, v_ref, out_ref, ids_ref, held, sems):
    width = QB * RANK
    rows = u_ref.shape[1]
    columns = out_ref.shape[2]
    per = LANES // width
    named = pltpu.make_async_copy(ids_hbm, ids_ref, sems.at[4])
    named.start()
    copies = [
        pltpu.make_async_copy(ref.at[layer], held.at[s], sems.at[s]) for s, ref in enumerate((u_ref, v_ref))
    ]
    for copy in copies:
        copy.start()
    named.wait()
    lane = lax.broadcasted_iota(jnp.int32, (rows, LANES), 1) // width
    for s in range(2):
        copies[s].wait()
        for chunk in range(columns // LANES):
            total = None
            for k in range(per):
                stored = ids_ref[layer, chunk * per + k]
                start = pl.multiple_of((stored // per) * LANES, LANES)
                part = held[s, :, pl.ds(start, LANES)].astype(jnp.float32)
                part = pltpu.roll(part, lax.rem(k - stored % per + per, per) * width, 1)
                total = part if total is None else jnp.where(lane == k, part, total)
            out_ref[s, :, chunk * LANES : (chunk + 1) * LANES] = total.astype(jnp.bfloat16)


def in_hbm(*arrays):
    return [pltpu.with_memory_space_constraint(one, pltpu.HBM) for one in arrays]


def pick(layer, query_u, query_v, block_ids):
    _, rows, bank = query_u.shape
    columns = block_ids.shape[1] * QB * RANK
    anywhere = pl.BlockSpec(memory_space=pltpu.HBM)
    return pl.pallas_call(
        functools.partial(pick_kernel, layer),
        out_shape=jax.ShapeDtypeStruct((2, rows, columns), jnp.bfloat16),
        in_specs=[anywhere] * 3,
        out_specs=pl.BlockSpec(memory_space=pltpu.VMEM),
        scratch_shapes=[
            pltpu.SMEM(block_ids.shape, jnp.int32),
            pltpu.VMEM((2, rows, bank), jnp.bfloat16),
            pltpu.SemaphoreType.DMA((5,)),
        ],
        compiler_params=pltpu.CompilerParams(vmem_limit_bytes=GRANT),
        cost_estimate=pl.CostEstimate(
            flops=4 * rows * columns, bytes_accessed=4 * rows * (bank + columns), transcendentals=0
        ),
    )(*in_hbm(block_ids, query_u, query_v))


def load_kernel(layer, *refs):
    half = (len(refs) - 2) // 2 if layer == 0 else (len(refs) - 1) // 2
    refs, sems = list(refs[:-1]), refs[-1]
    if layer == 0:
        counts_ref, live_ref = refs.pop(0), refs.pop(half)
    copies = [pltpu.make_async_copy(refs[i].at[layer], refs[half + i], sems.at[i]) for i in range(half)]
    for copy in copies:
        copy.start()
    if layer == 0:
        live_ref[...] = jnp.full(live_ref.shape, counts_ref[0], jnp.int32)
    for copy in copies:
        copy.wait()


def load(layer, counts, *arrays):
    outs = [jax.ShapeDtypeStruct((8, LANES), jnp.int32)] if layer == 0 else []
    outs += [jax.ShapeDtypeStruct(one.shape[1:], one.dtype) for one in arrays]
    specs = [pl.BlockSpec(memory_space=pltpu.SMEM)] if layer == 0 else []
    args = ([counts] if layer == 0 else []) + in_hbm(*arrays)
    return pl.pallas_call(
        functools.partial(load_kernel, layer),
        out_shape=tuple(outs),
        in_specs=specs + [pl.BlockSpec(memory_space=pltpu.HBM)] * len(arrays),
        out_specs=(pl.BlockSpec(memory_space=pltpu.VMEM),) * len(outs),
        scratch_shapes=[pltpu.SemaphoreType.DMA((len(arrays),))],
        compiler_params=pltpu.CompilerParams(vmem_limit_bytes=GRANT),
    )(*args)


def split_dot(left, right):
    total = None
    rest = left
    for _ in range(TERMS):
        term = rest.astype(jnp.bfloat16)
        rest = rest - term.astype(jnp.float32)
        part = jnp.dot(term, right, preferred_element_type=jnp.float32)
        total = part if total is None else total + part
    return total


def group_sums(columns):
    row = lax.broadcasted_iota(jnp.int32, (columns, LANES), 0)
    col = lax.broadcasted_iota(jnp.int32, (columns, LANES), 1)
    return jnp.where(row // RANK == col, 1.0, 0.0).astype(jnp.bfloat16)


def stage_kernel(cfg, *refs):
    shape, where, rows = cfg["shape"], cfg["where"], cfg["rows"]
    refs = list(refs)

    def take(n):
        return [refs.pop(0) for _ in range(n)]

    x_refs = take(2)
    pieces = [take(2) for _ in where]
    start = take(3) if cfg["carry"] else None
    total = take(3)
    w = take(1)[0]
    tiles = w.shape[2] // TILE
    spans = []
    for slot, (key, pair) in enumerate(zip(where, pieces)):
        spans.append(lay_out(shape, key, pair, rows, w, slot * 2 * rows))
    for slot, x_span in enumerate(spans):
        span = slice(slot * 2 * rows, (slot + 1) * 2 * rows)
        came = start if slot == 0 else total
        for s in range(2):
            part = jnp.dot(x_refs[s][:, x_span], w[s, span, :], preferred_element_type=jnp.float32)
            total[s][...] = part if came is None else came[s][...] + part
        for s in range(2):
            for t in range(tiles):
                one = w[s, span, t * TILE : (t + 1) * TILE]
                part = lax.dot_general(one, one, (((0,), (0,)), ((), ())), preferred_element_type=jnp.float32)
                i = s * tiles + t
                total[2][i] = part if came is None else came[2][i] + part


def lay_out(shape, key, pair, rows, w, base):
    outer, inner = shape
    da, db = key
    me = lax.axis_index("tok")
    a, b, c = me // (2 * inner), (me // 2) % inner, me % 2
    owner = ((a + outer - da) % outer) * inner + (b + inner - db) % inner
    for dc, array in enumerate(pair):
        spot = pl.multiple_of(base + ((c + dc) % 2) * rows, LANES)
        w[:, pl.ds(spot, rows), :] = array[...]
    return pl.ds(pl.multiple_of(owner * 2 * rows, LANES), 2 * rows)


def stage(shape, where, arrays, tokens, carry):
    rows, columns = arrays[0][0].shape[1:]
    count = tokens[0].shape[0]
    slots = len(where)
    tiles = 2 * (columns // TILE)
    args = list(tokens) + [piece for pair in arrays for piece in pair]
    aliases = {}
    if carry is not None:
        aliases = {len(args) + i: i for i in range(3)}
        args += list(carry)
    vmem = pl.BlockSpec(memory_space=pltpu.VMEM)
    proj = jax.ShapeDtypeStruct((count, columns), jnp.float32)
    cfg = dict(shape=shape, rows=rows, where=where, carry=carry is not None)
    return pl.pallas_call(
        functools.partial(stage_kernel, cfg),
        out_shape=(proj, proj, jax.ShapeDtypeStruct((tiles, TILE, TILE), jnp.float32)),
        in_specs=[vmem] * len(args),
        out_specs=(vmem,) * 3,
        scratch_shapes=[pltpu.VMEM((2, slots * 2 * rows, columns), jnp.bfloat16)],
        input_output_aliases=aliases,
        compiler_params=pltpu.CompilerParams(vmem_limit_bytes=GRANT),
        cost_estimate=pl.CostEstimate(
            flops=4 * slots * rows * columns * (2 * count + tiles * TILE),
            bytes_accessed=8 * slots * rows * (count + columns),
            transcendentals=0,
        ),
    )(*args)


def finish_kernel(cfg, *refs):
    shape, layers, tile, rows, key = cfg["shape"], cfg["layers"], cfg["tile"], cfg["rows"], cfg["key"]
    refs = list(refs)

    def take(n):
        return [refs.pop(0) for _ in range(n)]

    live_ref = take(1)[0]
    x_refs = [take(2) for _ in range(layers)]
    pieces = [take(2) for _ in range(layers)]
    carries = [take(3) for _ in range(layers)]
    if tile:
        take(1)
    out_ref, w, held, product, made, sem = take(6)
    cols = slice(tile * TILE, (tile + 1) * TILE)
    tiles = carries[0][2].shape[0] // 2
    spans = [lay_out(shape, key, pieces[n], rows, w.at[n], 0) for n in range(layers)]
    row = lax.broadcasted_iota(jnp.int32, (TILE, TILE), 0)
    col = lax.broadcasted_iota(jnp.int32, (TILE, TILE), 1)
    norm = None
    for n, carry in enumerate(carries):
        for s in range(2):
            part = jnp.dot(x_refs[n][s][:, spans[n]], w[n, s], preferred_element_type=jnp.float32)
            part = carry[s][:, cols] + part
            if s == 0:
                held[...] = part
            else:
                part = held[...] * part
                product[...] = part if n == 0 else product[...] + part
        grams = []
        for s in range(2):
            one = w[n, s]
            part = lax.dot_general(one, one, (((0,), (0,)), ((), ())), preferred_element_type=jnp.float32)
            grams.append(carry[2][s * tiles + tile] + part)
        both = grams[0] * grams[1]
        norm = both if norm is None else norm + both
    norm = jnp.sum(jnp.where(row // RANK == col // RANK, norm, 0.0), axis=0, keepdims=True)
    chooser = group_sums(TILE)
    norm = split_dot(jnp.broadcast_to(norm, (8, TILE)), chooser)[:1]
    scale = 1.0 / jnp.sqrt(norm + 1e-06)
    for low in range(0, product.shape[0], LANES):
        span = slice(low, low + LANES)
        rest, terms = product[span], []
        for _ in range(TERMS):
            terms.append(rest.astype(jnp.bfloat16))
            rest = rest - terms[-1].astype(jnp.float32)
        raw = jnp.dot(jnp.concatenate(terms, axis=0), chooser, preferred_element_type=jnp.float32)
        raw = sum(raw[i * LANES : (i + 1) * LANES] for i in range(TERMS))
        token = low + lax.broadcasted_iota(jnp.int32, raw.shape, 0)
        scaled = jnp.where(token < live_ref[:1], raw * scale, 0.0)
        made[:, span] = scaled.T[: TILE // RANK]
    out = pltpu.make_async_copy(made, out_ref.at[pl.ds(tile * (TILE // RANK), TILE // RANK), :], sem)
    out.start()
    out.wait()


def finish(shape, key, tile, arrays, tokens, carries, live, before):
    layers, rows = len(arrays), arrays[0][0].shape[1]
    count, columns = carries[0][0].shape
    args = [live] + [one for pair in tokens for one in pair] + [one for pair in arrays for one in pair]
    args += [one for carry in carries for one in carry]
    vmem, hbm = pl.BlockSpec(memory_space=pltpu.VMEM), pl.BlockSpec(memory_space=pltpu.HBM)
    specs, aliases = [vmem] * len(args), {}
    if tile:
        aliases = {len(args): 0}
        args.append(before)
        specs.append(hbm)
    cfg = dict(shape=shape, layers=layers, tile=tile, rows=rows, key=key)
    return pl.pallas_call(
        functools.partial(finish_kernel, cfg),
        out_shape=jax.ShapeDtypeStruct((columns // RANK, count), jnp.float32),
        in_specs=specs,
        out_specs=hbm,
        scratch_shapes=[
            pltpu.VMEM((layers, 2, 2 * rows, TILE), jnp.bfloat16),
            pltpu.VMEM((count, TILE), jnp.float32),
            pltpu.VMEM((count, TILE), jnp.float32),
            pltpu.VMEM((TILE // RANK, count), jnp.float32),
            pltpu.SemaphoreType.DMA,
        ],
        input_output_aliases=aliases,
        compiler_params=pltpu.CompilerParams(vmem_limit_bytes=GRANT),
        cost_estimate=pl.CostEstimate(
            flops=8 * layers * rows * TILE * count, bytes_accessed=8 * rows * count, transcendentals=0
        ),
    )(*args)


def after(value, *others):
    return lax.optimization_barrier((value,) + others)[0]


def per_device(shape, activations, gradients, query_u, query_v, block_ids, counts):
    outer, inner = shape

    def number(a, b, c):
        return ((a % outer) * inner + b % inner) * 2 + c % 2

    def move(value, da, db, dc):
        steps = [
            (number(a, b, c), number(a + da, b + db, c + dc))
            for a in range(outer)
            for b in range(inner)
            for c in range(2)
        ]
        return lax.ppermute(value, "tok", steps)

    have, pairs = [{}, {}], [{}, {}]
    for layer in range(2):
        have[layer][(0, 0)] = pick(layer, query_u, query_v, block_ids)
    for da in range(outer):
        for layer in range(2):
            h = have[layer]
            if da < outer - 1:
                fed = h[(da, 0)]
                h[(da + 1, 0)] = move(fed, 1, 0, 0)
            if da < outer - 1:
                h[(da, 1)] = move(h[(da, 0)], 0, 1, 0)
    end = (outer - 1, 1)
    tiles = have[0][(0, 0)].shape[2] // TILE
    ends = [[], []]
    for t in range(tiles):
        cut = slice(t * TILE, (t + 1) * TILE)
        across = have[0][(outer - 1, 0)]
        ends[1].append(move(after(have[1][(0, 1)][:, :, cut], across), -1, 0, 0))
        ends[0].append(move(across[:, :, cut], 0, 1, 0))
    for layer in range(2):
        for key, piece in have[layer].items():
            pairs[layer][key] = [piece, move(piece, 0, 0, 1)]

    live, *first = load(0, counts, gradients, activations)
    tokens = [first, load(1, counts, gradients, activations)]

    parts = [[(0, 0), (0, 1), (1, 0)]] + [[(da, 1), (da + 1, 0)] for da in range(1, outer - 1)]
    carry = [None, None]
    for keys in parts:
        for layer in range(2):
            arrays = [pairs[layer][one] for one in keys]
            carry[layer] = stage(shape, keys, arrays, tokens[layer], carry[layer])
    scores = None
    for t in range(tiles):
        arrays = [[ends[layer][t], move(ends[layer][t], 0, 0, 1)] for layer in range(2)]
        scores = finish(shape, end, t, arrays, tokens, carry, live, scores)
    return scores.T


def solution(mesh):
    spec = (
        P(None, ("groups", "tok"), None),
        P(None, ("groups", "tok"), None),
        P("groups", "tok", None),
        P("groups", "tok", None),
        P("groups", None),
        P(("groups", "tok")),
    )
    members = mesh.shape["tok"]
    shape = (OUTER, members // (2 * OUTER))
    ring = members == 4 * OUTER

    def body(*args):
        fits = ring and args[2].shape[1] % LANES == 0
        return per_device(shape, *args) if fits else per_device_plain(*args)

    return jax.shard_map(body, mesh=mesh, in_specs=spec, out_specs=P(("groups", "tok"), None), check_vma=False)
```

```python
import functools

import jax
import jax.numpy as jnp
from jax import lax
from jax.experimental import pallas as pl
from jax.experimental.pallas import tpu as pltpu
from jax.sharding import PartitionSpec as P


RANK = 8
QB = 4
OUTER = 4
LANES = 128
TILE = 256
TERMS = 2
GRANT = 24 << 20


def pick_columns(factor, block_ids):
    width = QB * RANK
    chosen = []
    for layer in range(factor.shape[0]):
        slots = factor[layer].reshape(factor.shape[1], -1, width)
        chosen.append(jnp.take(slots, block_ids[layer], axis=1).reshape(factor.shape[1], -1))
    return jnp.stack(chosen)


def rank_grams(factor):
    per = factor.reshape(factor.shape[0], factor.shape[1], -1, RANK)
    return jnp.einsum("lkqr,lkqs->lqrs", per, per, preferred_element_type=jnp.float32)


def per_device_plain(activations, gradients, query_u, query_v, block_ids, counts):
    layers, tok_rows, _ = activations.shape
    columns = block_ids.shape[1] * QB * RANK
    queries = columns // RANK
    whole_u = lax.all_gather(pick_columns(query_u, block_ids), "tok", axis=1, tiled=True)
    whole_v = lax.all_gather(pick_columns(query_v, block_ids), "tok", axis=1, tiled=True)
    grad_proj = jnp.einsum("ltk,lkc->ltc", gradients, whole_u, preferred_element_type=jnp.float32)
    act_proj = jnp.einsum("ltk,lkc->ltc", activations, whole_v, preferred_element_type=jnp.float32)
    raw = jnp.sum((grad_proj * act_proj).reshape(layers, tok_rows, queries, RANK), axis=(0, 3))
    norm_sq = jnp.sum(rank_grams(whole_u) * rank_grams(whole_v), axis=(0, 2, 3))
    live = jnp.arange(tok_rows, dtype=jnp.int32) < counts[0]
    scaled = raw / jnp.sqrt(norm_sq + 1e-06)[None, :]
    return jnp.where(live[:, None], scaled, jnp.zeros_like(scaled))


def pick_kernel(layer, ids_hbm, u_ref, v_ref, out_ref, ids_ref, held, sems):
    width = QB * RANK
    rows = u_ref.shape[1]
    columns = out_ref.shape[2]
    per = LANES // width
    named = pltpu.make_async_copy(ids_hbm, ids_ref, sems.at[4])
    named.start()
    copies = [
        pltpu.make_async_copy(ref.at[layer], held.at[s], sems.at[s]) for s, ref in enumerate((u_ref, v_ref))
    ]
    for copy in copies:
        copy.start()
    named.wait()
    lane = lax.broadcasted_iota(jnp.int32, (rows, LANES), 1) // width
    for copy in copies:
        copy.wait()
    for s in range(2):
        for chunk in range(columns // LANES):
            total = None
            for k in range(per):
                stored = ids_ref[layer, chunk * per + k]
                start = pl.multiple_of((stored // per) * LANES, LANES)
                part = held[s, :, pl.ds(start, LANES)]
                part = pltpu.roll(part, lax.rem(k - stored % per + per, per) * width, 1)
                total = part if total is None else jnp.where(lane == k, part, total)
            out_ref[s, :, chunk * LANES : (chunk + 1) * LANES] = total


def in_hbm(*arrays):
    return [pltpu.with_memory_space_constraint(one, pltpu.HBM) for one in arrays]


def pick(layer, query_u, query_v, block_ids):
    _, rows, bank = query_u.shape
    columns = block_ids.shape[1] * QB * RANK
    anywhere = pl.BlockSpec(memory_space=pltpu.HBM)
    return pl.pallas_call(
        functools.partial(pick_kernel, layer),
        out_shape=jax.ShapeDtypeStruct((2, rows, columns), jnp.bfloat16),
        in_specs=[anywhere] * 3,
        out_specs=pl.BlockSpec(memory_space=pltpu.VMEM),
        scratch_shapes=[
            pltpu.SMEM(block_ids.shape, jnp.int32),
            pltpu.VMEM((2, rows, bank), jnp.bfloat16),
            pltpu.SemaphoreType.DMA((5,)),
        ],
        compiler_params=pltpu.CompilerParams(vmem_limit_bytes=GRANT),
        cost_estimate=pl.CostEstimate(
            flops=4 * rows * columns, bytes_accessed=4 * rows * (bank + columns), transcendentals=0
        ),
    )(*in_hbm(block_ids, query_u, query_v))


def load_kernel(layer, *refs):
    half = (len(refs) - 2) // 2 if layer == 0 else (len(refs) - 1) // 2
    refs, sems = list(refs[:-1]), refs[-1]
    if layer == 0:
        counts_ref, live_ref = refs.pop(0), refs.pop(half)
    copies = [pltpu.make_async_copy(refs[i].at[layer], refs[half + i], sems.at[i]) for i in range(half)]
    for copy in copies:
        copy.start()
    if layer == 0:
        live_ref[...] = jnp.full(live_ref.shape, counts_ref[0], jnp.int32)
    for copy in copies:
        copy.wait()


def load(layer, counts, *arrays):
    outs = [jax.ShapeDtypeStruct((8, LANES), jnp.int32)] if layer == 0 else []
    outs += [jax.ShapeDtypeStruct(one.shape[1:], one.dtype) for one in arrays]
    specs = [pl.BlockSpec(memory_space=pltpu.SMEM)] if layer == 0 else []
    args = ([counts] if layer == 0 else []) + in_hbm(*arrays)
    return pl.pallas_call(
        functools.partial(load_kernel, layer),
        out_shape=tuple(outs),
        in_specs=specs + [pl.BlockSpec(memory_space=pltpu.HBM)] * len(arrays),
        out_specs=(pl.BlockSpec(memory_space=pltpu.VMEM),) * len(outs),
        scratch_shapes=[pltpu.SemaphoreType.DMA((len(arrays),))],
        compiler_params=pltpu.CompilerParams(vmem_limit_bytes=GRANT),
    )(*args)


def split_dot(left, right):
    total = None
    rest = left
    for _ in range(TERMS):
        term = rest.astype(jnp.bfloat16)
        rest = rest - term.astype(jnp.float32)
        part = jnp.dot(term, right, preferred_element_type=jnp.float32)
        total = part if total is None else total + part
    return total


def group_sums(columns):
    row = lax.broadcasted_iota(jnp.int32, (columns, LANES), 0)
    col = lax.broadcasted_iota(jnp.int32, (columns, LANES), 1)
    return jnp.where(row // RANK == col, 1.0, 0.0).astype(jnp.bfloat16)


def stage_kernel(cfg, *refs):
    (outer, inner), groups, last, rows = cfg["shape"], cfg["groups"], cfg["last"], cfg["rows"]
    refs = list(refs)

    def take(n):
        return [refs.pop(0) for _ in range(n)]

    x_refs = [take(2) for _ in groups]
    live_ref = take(1)[0] if last else None
    pieces = [[take(2) for _ in g["where"]] for g in groups]
    starts = [take(3) if g["carry"] else None for g in groups]
    outs = take(1) if last else None
    product = take(1)[0] if last else None
    totals = [take(3) for _ in groups]
    w = take(1)[0]
    me = lax.axis_index("tok")
    a, b, c = me // (2 * inner), (me // 2) % inner, me % 2
    spans, slot = [], 0
    for g, arrays in zip(groups, pieces):
        for (da, db), pair in zip(g["where"], arrays):
            owner = ((a + outer - da) % outer) * inner + (b + inner - db) % inner
            start = pl.multiple_of(owner * 2 * rows, LANES)
            for dc, array in enumerate(pair):
                spot = pl.multiple_of(slot * 2 * rows + ((c + dc) % 2) * rows, LANES)
                w[:, pl.ds(spot, rows), :] = array[...]
            spans.append(pl.ds(start, 2 * rows))
            slot += 1
    tiles = w.shape[2] // TILE
    slot = 0
    for n, (g, start, total) in enumerate(zip(groups, starts, totals)):
        for first in range(len(g["where"])):
            span = slice(slot * 2 * rows, (slot + 1) * 2 * rows)
            came = start if first == 0 else total
            for s in range(2):
                x = x_refs[n][s][:, spans[slot]]
                part = jnp.dot(x, w[s, span, :], preferred_element_type=jnp.float32)
                if came is not None:
                    part = came[s][...] + part
                if last and s == 1:
                    part = total[0][...] * part
                    product[...] = part if g is groups[0] else product[...] + part
                else:
                    total[s][...] = part
            for s in range(2):
                for t in range(tiles):
                    one = w[s, span, t * TILE : (t + 1) * TILE]
                    part = lax.dot_general(one, one, (((0,), (0,)), ((), ())), preferred_element_type=jnp.float32)
                    i = s * tiles + t
                    total[2][i] = part if came is None else came[2][i] + part
            slot += 1
    if last:
        columns = w.shape[2]
        row = lax.broadcasted_iota(jnp.int32, (TILE, TILE), 0)
        col = lax.broadcasted_iota(jnp.int32, (TILE, TILE), 1)
        same = row // RANK == col // RANK
        norm = []
        for t in range(tiles):
            both = sum(total[2][t] * total[2][tiles + t] for total in totals)
            norm.append(jnp.sum(jnp.where(same, both, 0.0), axis=0, keepdims=True))
        norm = jnp.broadcast_to(jnp.concatenate(norm, axis=1), (8, columns))
        chooser = group_sums(columns)
        scale = 1.0 / jnp.sqrt(split_dot(norm, chooser)[:1] + 1e-06)
        tokens = product.shape[0]
        for low in range(0, tokens, LANES):
            span = slice(low, low + LANES)
            rest, terms = product[span], []
            for _ in range(TERMS):
                terms.append(rest.astype(jnp.bfloat16))
                rest = rest - terms[-1].astype(jnp.float32)
            raw = jnp.dot(jnp.concatenate(terms, axis=0), chooser, preferred_element_type=jnp.float32)
            raw = sum(raw[i * LANES : (i + 1) * LANES] for i in range(TERMS))
            token = low + lax.broadcasted_iota(jnp.int32, raw.shape, 0)
            scaled = jnp.where(token < live_ref[:1], raw * scale, 0.0)
            outs[0][:, span] = scaled.T[: columns // RANK]


def stage(shape, groups, live=None):
    last = live is not None
    rows, columns = groups[0]["arrays"][0][0].shape[1:]
    tokens = groups[0]["tokens"][0].shape[0]
    slots = sum(len(g["where"]) for g in groups)
    tiles = 2 * (columns // TILE)
    vmem = pl.BlockSpec(memory_space=pltpu.VMEM)
    args, specs = [], []
    for g in groups:
        args += g["tokens"]
        specs += [vmem] * 2
    if last:
        args.append(live)
        specs.append(vmem)
    for g in groups:
        for pair in g["arrays"]:
            args += pair
            specs += [vmem] * 2
    aliases = {}
    for n, g in enumerate(groups):
        if g["carry"] is not None:
            if not last:
                aliases.update({len(args) + i: 3 * n + i for i in range(3)})
            args += list(g["carry"])
            specs += [vmem] * 3
    sums = [((tokens, columns), jnp.float32)] * 2 + [((tiles, TILE, TILE), jnp.float32)]
    scratch = []
    if last:
        out_shape = jax.ShapeDtypeStruct((columns // RANK, tokens), jnp.float32)
        out_specs = vmem
        scratch = [pltpu.VMEM(*sums[0])] + [pltpu.VMEM(*one) for one in sums] * len(groups)
    else:
        out_shape = tuple(jax.ShapeDtypeStruct(*one) for one in sums) * len(groups)
        out_specs = (vmem,) * len(out_shape)
    cfg = dict(
        shape=shape,
        rows=rows,
        last=last,
        groups=[dict(layer=g["layer"], where=g["where"], carry=g["carry"] is not None) for g in groups],
    )
    flops = 4 * slots * rows * columns * (2 * tokens + tiles * TILE)
    return pl.pallas_call(
        functools.partial(stage_kernel, cfg),
        out_shape=out_shape,
        in_specs=specs,
        out_specs=out_specs,
        scratch_shapes=scratch + [pltpu.VMEM((2, slots * 2 * rows, columns), jnp.bfloat16)],
        input_output_aliases=aliases,
        compiler_params=pltpu.CompilerParams(vmem_limit_bytes=GRANT),
        cost_estimate=pl.CostEstimate(
            flops=flops, bytes_accessed=8 * slots * rows * (tokens + columns), transcendentals=0
        ),
    )(*args)


def after(value, *others):
    return lax.optimization_barrier((value,) + others)[0]


def per_device(shape, activations, gradients, query_u, query_v, block_ids, counts):
    outer, inner = shape

    def number(a, b, c):
        return ((a % outer) * inner + b % inner) * 2 + c % 2

    def move(value, da, db, dc):
        steps = [
            (number(a, b, c), number(a + da, b + db, c + dc))
            for a in range(outer)
            for b in range(inner)
            for c in range(2)
        ]
        return lax.ppermute(value, "tok", steps)

    have, pairs = [{}, {}], [{}, {}]
    for layer in range(2):
        have[layer][(0, 0)] = pick(layer, query_u, query_v, block_ids)
    for da in range(outer):
        for layer in range(2):
            h = have[layer]
            if da < outer - 1:
                fed = h[(da, 0)]
                h[(da + 1, 0)] = move(fed, 1, 0, 0)
            if da == outer - 1 and layer == 1:
                fed = after(h[(0, 1)], have[0][(da, 0)])
                h[(da, 1)] = move(fed, -1, 0, 0)
            else:
                h[(da, 1)] = move(h[(da, 0)], 0, 1, 0)
    for layer in range(2):
        for key, piece in have[layer].items():
            pairs[layer][key] = [piece, move(piece, 0, 0, 1)]

    live, *first = load(0, counts, gradients, activations)
    tokens = [first, load(1, counts, gradients, activations)]

    def group(layer, keys, carry):
        return dict(layer=layer, where=keys, arrays=[pairs[layer][key] for key in keys], carry=carry, tokens=tokens[layer])

    parts = [[(0, 0), (0, 1), (1, 0)]] + [[(da, 1), (da + 1, 0)] for da in range(1, outer - 1)]
    carry = [None, None]
    for keys in parts:
        for layer in range(2):
            carry[layer] = stage(
                shape, [group(layer, keys, carry[layer])])
    scores = stage(shape, [group(layer, [(outer - 1, 1)], carry[layer]) for layer in range(2)], live=live)
    return scores.T


def solution(mesh):
    spec = (
        P(None, ("groups", "tok"), None),
        P(None, ("groups", "tok"), None),
        P("groups", "tok", None),
        P("groups", "tok", None),
        P("groups", None),
        P(("groups", "tok")),
    )
    members = mesh.shape["tok"]
    shape = (OUTER, members // (2 * OUTER))
    ring = members == 4 * OUTER

    def body(*args):
        fits = ring and args[2].shape[1] % LANES == 0
        return per_device(shape, *args) if fits else per_device_plain(*args)

    return jax.shard_map(body, mesh=mesh, in_specs=spec, out_specs=P(("groups", "tok"), None), check_vma=False)
```
